32 devices in a mesh: row: 4 (over y, x), col: 8 (over z, core).
Axes of the slice: x: 2, y: 2, z: 4, core: 2. Of those that a mesh axis runs over, the one named last changes fastest.
Arguments:
- covariance: float32 [64, 128, 64, 128], P('row', None, 'col'), may hold values from -1 to 4, as said below
- wind_x: float32 [64, 128], replicated, may hold values from -0.2 to 0.2
- wind_y: float32 [64, 128], replicated, may hold values from -0.2 to 0.2
- diffusivity: float32 [64, 128], replicated, may hold values from 0.1 to 0.2
- obs_point: int32 [512], replicated, may hold values from 0 to 8191, as said below
- obs_var: float32 [512], replicated, may hold values from 0.3 to 1
Outputs:
- analysis: float32 [64, 128, 64, 128], P('row', None, 'col')
The draws below stay inside these ranges and needn't reach their ends.
Inputs may be any that keep to these rules, and one draw needn't show every extreme that they name: `covariance`: symmetric and positive definite. `obs_point`: distinct and ascending; at most 128 of them lie in one aligned block of 1024 points and some block holds exactly 128; at most 256 lie in one aligned block of 2048 points and some block holds exactly 256.
All inputs are finite; a program needn't handle non-finite values.
Results may differ from the reference program's by a relative error of at most 0.0001.
Values sent between devices are 32-bit elements; how exact they have to be, the bound alone decides.
A program may use at most 128 MiB of HBM per device.

```python
import math
import jax
import jax.numpy as jnp
from jax import lax

GY = 64
GX = 128
NOBS = 512
STEPS = 2
NS_ITERS = 4
NPTS = 8192
ROWS_DEV = 2048
COLS_DEV = 1024
MAXC = 128


def draw_covariance(key, part):
    noise_key, diag_key = jax.random.split(jax.random.fold_in(key, 11))
    noise = jax.random.normal(noise_key, (GY, GX, GY, GX), jnp.float32)
    symmetric = (noise + noise.transpose(2, 3, 0, 1)) * (0.25 / math.sqrt(GY * GX))
    diagonal = jax.random.uniform(diag_key, (GY, GX), jnp.float32, 1.0, 3.0)
    same_y = jnp.arange(GY)[:, None, None, None] == jnp.arange(GY)[None, None, :, None]
    same_x = jnp.arange(GX)[None, :, None, None] == jnp.arange(GX)[None, None, None, :]
    identity = (same_y & same_x).astype(jnp.float32)
    return symmetric + identity * diagonal[:, :, None, None]


def draw_obs_point(key, part):
    full_key, slot_key, point_key = jax.random.split(jax.random.fold_in(key, 7), 3)
    col_blocks = NPTS // COLS_DEV
    row_blocks = NPTS // ROWS_DEV
    per_row = col_blocks // row_blocks
    full_row = jax.random.randint(full_key, (), 0, row_blocks)
    slot_block = jnp.arange(col_blocks * MAXC, dtype=jnp.int32) // MAXC
    slot_full = slot_block // per_row == full_row
    score = jax.random.permutation(slot_key, col_blocks * MAXC).astype(jnp.int32)
    score = jnp.where(slot_full, -1, score)
    order = jnp.argsort(score, stable=True)
    taken = jnp.zeros((col_blocks * MAXC,), jnp.int32).at[order[:NOBS]].set(1)
    block_counts = jnp.sum(taken.reshape(col_blocks, MAXC), axis=1)
    limit = 2 ** 30 // COLS_DEV
    point_score = jax.random.randint(point_key, (col_blocks, COLS_DEV), 0, limit) * COLS_DEV + jnp.arange(COLS_DEV, dtype=jnp.int32)[None, :]
    ranks = jnp.argsort(jnp.argsort(point_score, axis=1), axis=1)
    chosen = (ranks < block_counts[:, None]).reshape(-1)
    return jnp.nonzero(chosen, size=NOBS)[0].astype(jnp.int32)


def setup_inputs(seed: int = 0) -> dict:
    keys = jax.random.split(jax.random.key(seed), 7)
    covariance = draw_covariance(jax.random.fold_in(keys[6], 71), 0)
    wind_x = jnp.clip(jax.random.uniform(keys[1], (GY, GX), jnp.float32, -0.2, 0.2), -0.2, 0.2)
    wind_y = jnp.clip(jax.random.uniform(keys[2], (GY, GX), jnp.float32, -0.2, 0.2), -0.2, 0.2)
    diffusivity = jnp.clip(jax.random.uniform(keys[3], (GY, GX), jnp.float32, 0.1, 0.2), 0.1, 0.2)
    obs_point = draw_obs_point(jax.random.fold_in(keys[6], 71), 0)
    obs_var = jnp.clip(jnp.exp(jax.random.uniform(keys[5], (NOBS,), jnp.float32, math.log(0.3), math.log(1.0))), 0.3, 1.0)
    return dict(covariance=covariance, wind_x=wind_x, wind_y=wind_y, diffusivity=diffusivity, obs_point=obs_point, obs_var=obs_var)


newton_scale = 4.0


def stencil_weights(wind_x, wind_y, diffusivity):
    return (1.0 - 4.0 * diffusivity, diffusivity - 0.5 * wind_x, diffusivity + 0.5 * wind_x,
            diffusivity - 0.5 * wind_y, diffusivity + 0.5 * wind_y)


def apply_first(extended, weights):
    inner = extended[1:-1]
    w_centre, w_east, w_west, w_north, w_south = [w_table[1:-1, :, None, None] for w_table in weights]
    return (w_centre * inner + w_east * jnp.roll(inner, -1, axis=1) + w_west * jnp.roll(inner, 1, axis=1)
            + w_north * extended[2:] + w_south * extended[:-2])


def apply_second(extended, weights):
    inner = extended[:, :, 1:-1]
    w_centre, w_east, w_west, w_north, w_south = [w_table[None, None, 1:-1, :] for w_table in weights]
    return (w_centre * inner + w_east * jnp.roll(inner, -1, axis=3) + w_west * jnp.roll(inner, 1, axis=3)
            + w_north * extended[:, :, 2:] + w_south * extended[:, :, :-2])


def reference(covariance, wind_x, wind_y, diffusivity, obs_point, obs_var):
    padded = tuple(jnp.pad(w_table, ((1, 1), (0, 0))) for w_table in stencil_weights(wind_x, wind_y, diffusivity))
    transported = covariance
    for step_index in range(STEPS):
        transported = apply_first(jnp.pad(transported, ((1, 1), (0, 0), (0, 0), (0, 0))), padded)
        transported = apply_second(jnp.pad(transported, ((0, 0), (0, 0), (1, 1), (0, 0))), padded)
    flat_matrix = transported.reshape(NPTS, NPTS)
    obs_rows = jnp.take(flat_matrix, obs_point, axis=0)
    obs_cols = jnp.take(flat_matrix, obs_point, axis=1)
    innovation = jnp.take(obs_rows, obs_point, axis=1) + jnp.diag(obs_var)
    inverse = jnp.eye(NOBS, dtype=jnp.float32) / newton_scale
    for sweep_index in range(NS_ITERS):
        product = jnp.dot(innovation, inverse, precision=lax.Precision.HIGHEST)
        inverse = 2.0 * inverse - jnp.dot(inverse, product, precision=lax.Precision.HIGHEST)
    gain = jnp.dot(obs_cols, inverse, precision=lax.Precision.HIGHEST)
    analysis = flat_matrix - jnp.dot(gain, obs_rows, precision=lax.Precision.HIGHEST)
    return analysis.reshape(GY, GX, GY, GX)
```

```python
import functools

import jax
import jax.numpy as jnp
from jax import lax
from jax.experimental import pallas as pl
from jax.experimental.pallas import tpu as pltpu
from jax.sharding import PartitionSpec as P

STEPS = 2
NS_ITERS = 4
newton_scale = 4.0
HALO = STEPS
MESH = pl.DeviceIdType.MESH
NEAR = ((-1, 0), (1, 0), (0, -1), (0, 1), (-1, -1), (-1, 1), (1, -1), (1, 1))


def stencil_weights(wind_x, wind_y, diffusivity):
    return (
        1.0 - 4.0 * diffusivity,
        diffusivity - 0.5 * wind_x,
        diffusivity + 0.5 * wind_x,
        diffusivity - 0.5 * wind_y,
        diffusivity + 0.5 * wind_y,
    )


def split(value):
    high = value.astype(jnp.bfloat16)
    return high, (value - high.astype(jnp.float32)).astype(jnp.bfloat16)


def transport_kernel(
    sizes,
    row_ids,
    x_hbm,
    w1_ref,
    w2_ref,
    col_loc,
    flat_ref,
    rows_ref,
    cols_ref,
    ext,
    side,
    mid,
    one,
    w2b,
    local_sem,
    send_sem,
    recv_sem,
):
    row_count, col_count, ny, gx, nj = sizes
    row, col = lax.axis_index("row"), lax.axis_index("col")
    pts = ny * gx
    edge = HALO * gx
    pitch = gx + 16

    def there(dy, dx):
        return (
            (row + dy >= 0) & (row + dy < row_count) & (col + dx >= 0) & (col + dx < col_count)
        )

    load = pltpu.make_async_copy(x_hbm, ext.at[pl.ds(edge, pts)], local_sem)
    load.start()

    barrier = pltpu.get_barrier_semaphore()
    waits = 0
    for dy, dx in NEAR:
        here = there(dy, dx)

        @pl.when(here)
        def _(dy=dy, dx=dx):
            pl.semaphore_signal(
                barrier, inc=1, device_id=(row + dy, col + dx), device_id_type=MESH
            )

        waits = waits + here.astype(jnp.int32)

    def copies(slot, dy, dx):
        src_y = {-1: 0, 0: 0, 1: pts - edge}[dy]
        dst_y = {-1: edge + pts, 0: edge, 1: 0}[dy]
        length = pts if dy == 0 else edge
        target = (row + dy, col + dx)
        if dx == 0:
            pairs = [(x_hbm.at[pl.ds(src_y, length)], ext.at[pl.ds(dst_y, length)])]
        else:
            first = nj - HALO if dx > 0 else 0
            at = 0 if dx > 0 else HALO
            pairs = [
                (
                    x_hbm.at[pl.ds(src_y, length), first + k, :],
                    side.at[at + k, pl.ds(dst_y, length), :],
                )
                for k in range(HALO)
            ]
        return [
            pltpu.make_async_remote_copy(
                src_ref=src,
                dst_ref=dst,
                send_sem=send_sem.at[slot, k],
                recv_sem=recv_sem.at[slot, k],
                device_id=target,
                device_id_type=MESH,
            )
            for k, (src, dst) in enumerate(pairs)
        ]

    @pl.when(row == 0)
    def _():
        ext[pl.ds(0, edge)] = jnp.zeros((edge, nj, gx), jnp.float32)
        side[:, pl.ds(0, edge), :] = jnp.zeros((2 * HALO, edge, gx), jnp.float32)

    @pl.when(row == row_count - 1)
    def _():
        ext[pl.ds(edge + pts, edge)] = jnp.zeros((edge, nj, gx), jnp.float32)
        side[:, pl.ds(edge + pts, edge), :] = jnp.zeros((2 * HALO, edge, gx), jnp.float32)

    @pl.when(col == 0)
    def _():
        side[pl.ds(0, HALO)] = jnp.zeros((HALO, pts + 2 * edge, gx), jnp.float32)

    @pl.when(col == col_count - 1)
    def _():
        side[pl.ds(HALO, HALO)] = jnp.zeros((HALO, pts + 2 * edge, gx), jnp.float32)

    pl.semaphore_wait(barrier, waits)
    for slot, (dy, dx) in enumerate(NEAR):

        @pl.when(there(dy, dx))
        def _(slot=slot, dy=dy, dx=dx):
            for copy in copies(slot, dy, dx):
                copy.start()

    for k in range(5 * (nj + 2)):
        w2b[k] = jnp.broadcast_to(w2_ref[k : k + 1, :], (8, gx))
    load.wait()

    def arrive(slots):
        for slot in slots:
            dy, dx = NEAR[slot]

            @pl.when(there(-dy, -dx))
            def _(slot=slot, dy=dy, dx=dx):
                for copy in copies(slot, dy, dx):
                    copy.wait_recv()

    deep = 16

    def second_rows(y):
        def group(g, carry):
            at = pl.multiple_of(y * gx + g * deep, deep)
            values = [side[k, pl.ds(at, deep), :] for k in range(HALO)]
            values += [ext[pl.ds(at, deep), j, :] for j in range(nj)]
            values += [side[HALO + k, pl.ds(at, deep), :] for k in range(HALO)]
            for step in range(STEPS):
                new = []
                for j in range(1, len(values) - 1):
                    w = [
                        jnp.broadcast_to(
                            w2b[k * (nj + 2) + step + j - 1][None], (deep // 8, 8, gx)
                        ).reshape(deep, gx)
                        for k in range(5)
                    ]
                    v = values[j]
                    new.append(
                        w[0] * v
                        + w[1] * pltpu.roll(v, gx - 1, axis=1)
                        + w[2] * pltpu.roll(v, 1, axis=1)
                        + w[3] * values[j + 1]
                        + w[4] * values[j - 1]
                    )
                values = new
            to = pl.multiple_of(y * pitch + 8 + g * deep, 8)
            for j in range(nj):
                mid[j, pl.ds(to, deep), :] = values[j]
            return carry

        lax.fori_loop(0, gx // deep, group, 0)
        base = pl.multiple_of(y * pitch, 8)
        for j in range(nj):
            mid[j, pl.ds(base, 8), :] = mid[j, pl.ds(base + gx, 8), :]
            mid[j, pl.ds(base + 8 + gx, 8), :] = mid[j, pl.ds(base + 8, 8), :]

    def first_row(source, target, y, weight_y, to_base):
        def group(g, carry):
            at = pl.multiple_of(y * pitch + 8 + g * 8, 8)
            table = w1_ref[pl.ds(pl.multiple_of(weight_y * gx + g * 8, 8), 8), :]
            w = [jnp.broadcast_to(table[:, k : k + 1], (8, gx)) for k in range(5)]
            to = pl.multiple_of(to_base + g * 8, 8)
            for j in range(nj):
                target[j, pl.ds(to, 8), :] = (
                    w[0] * source[j, pl.ds(at, 8), :]
                    + w[1] * source[j, pl.ds(at + 1, 8), :]
                    + w[2] * source[j, pl.ds(at - 1, 8), :]
                    + w[3] * source[j, pl.ds(at + pitch, 8), :]
                    + w[4] * source[j, pl.ds(at - pitch, 8), :]
                )
            return carry

        lax.fori_loop(0, gx // 8, group, 0)

    def wrap(source, y):
        base = pl.multiple_of(y * pitch, 8)
        for j in range(nj):
            source[j, pl.ds(base, 8), :] = source[j, pl.ds(base + gx, 8), :]
            source[j, pl.ds(base + 8 + gx, 8), :] = source[j, pl.ds(base + 8, 8), :]

    def loop(low, high, body):
        def step(y, carry):
            body(y)
            return carry

        lax.fori_loop(low, high, step, 0)

    def one_row(y):
        first_row(mid, one, y + 1, y, y * pitch + 8)
        wrap(one, y)

    def two_row(y):
        first_row(one, flat_ref, y + 1, y + 1, y * gx)

    arrive((2, 3))
    loop(HALO, HALO + ny, second_rows)
    arrive((0, 1, 4, 5, 6, 7))
    loop(0, HALO, second_rows)
    loop(HALO + ny, 2 * HALO + ny, second_rows)
    loop(0, ny + 2, one_row)
    loop(0, ny, two_row)

    def pick(k, carry):
        at = row_ids[k]
        for j in range(nj):
            rows_ref[j, pl.ds(k, 1), :] = flat_ref[j, pl.ds(at, 1), :]
        return carry

    lax.fori_loop(0, rows_ref.shape[1], pick, 0)

    slots = cols_ref.shape[0]
    hots = []
    for j in range(nj):
        lane = lax.broadcasted_iota(jnp.int32, (slots, gx), 1) + j * gx
        hots.append((lane == col_loc[...]).astype(jnp.float32).astype(jnp.bfloat16))
    hot = jnp.concatenate(hots, axis=1)
    dims = (((1,), (1,)), ((), ()))

    def pick_cols(y, carry):
        at = pl.multiple_of(y * gx, gx)
        value = jnp.concatenate([flat_ref[j, pl.ds(at, gx), :] for j in range(nj)], axis=1)
        high, low = split(value)
        cols_ref[:, pl.ds(at, gx)] = lax.dot_general(
            hot, high, dims, preferred_element_type=jnp.float32
        ) + lax.dot_general(hot, low, dims, preferred_element_type=jnp.float32)
        return carry

    lax.fori_loop(0, ny, pick_cols, 0)

    for slot, (dy, dx) in enumerate(NEAR):

        @pl.when(there(dy, dx))
        def _(slot=slot, dy=dy, dx=dx):
            for copy in copies(slot, dy, dx):
                copy.wait_send()


def transport(tile, w1, w2, row_loc, col_loc, sizes):
    row_count, col_count, ny, gx, nj = sizes
    pts, edge, pitch = ny * gx, HALO * gx, gx + 16
    max_row, max_col = row_loc.shape[0], col_loc.shape[0]
    vmem = pl.BlockSpec(memory_space=pltpu.VMEM)
    return pl.pallas_call(
        functools.partial(transport_kernel, sizes),
        in_specs=[
            pl.BlockSpec(memory_space=pltpu.SMEM),
            pl.BlockSpec(memory_space=pl.ANY),
            vmem,
            vmem,
            vmem,
        ],
        out_specs=[vmem, vmem, vmem],
        out_shape=[
            jax.ShapeDtypeStruct((nj, pts, gx), jnp.float32),
            jax.ShapeDtypeStruct((nj, max_row, gx), jnp.float32),
            jax.ShapeDtypeStruct((max_col, pts), jnp.float32),
        ],
        scratch_shapes=[
            pltpu.VMEM((pts + 2 * edge, nj, gx), jnp.float32),
            pltpu.VMEM((2 * HALO, pts + 2 * edge, gx), jnp.float32),
            pltpu.VMEM((nj, (ny + 4) * pitch, gx), jnp.float32),
            pltpu.VMEM((nj, (ny + 2) * pitch, gx), jnp.float32),
            pltpu.VMEM((5 * (nj + 2), 8, gx), jnp.float32),
            pltpu.SemaphoreType.DMA(()),
            pltpu.SemaphoreType.DMA((8, HALO)),
            pltpu.SemaphoreType.DMA((8, HALO)),
        ],
        compiler_params=pltpu.CompilerParams(
            collective_id=0, has_side_effects=True, vmem_limit_bytes=62 << 20
        ),
    )(row_loc, tile, w1, w2, col_loc)


def update_kernel(nj, gx, rows, flat_ref, left_ref, right_ref, out_ref):
    left = left_ref[...].T
    l_hi, l_lo = split(left)
    wide = min(2, nj)
    for j in range(0, nj, wide):
        r_hi, r_lo = split(right_ref[:, j * gx : (j + wide) * gx])
        total = (
            jnp.dot(l_hi, r_hi, preferred_element_type=jnp.float32)
            + jnp.dot(l_hi, r_lo, preferred_element_type=jnp.float32)
            + jnp.dot(l_lo, r_hi, preferred_element_type=jnp.float32)
        )
        for k in range(wide):
            out_ref[:, j + k, :] = flat_ref[j + k] - total[:, k * gx : (k + 1) * gx]


def update(flat, left, right, rows):
    nj, pts, gx = flat.shape
    depth = left.shape[0]
    return pl.pallas_call(
        functools.partial(update_kernel, nj, gx, rows),
        grid=(pts // rows,),
        in_specs=[
            pl.BlockSpec((nj, rows, gx), lambda i: (0, i, 0)),
            pl.BlockSpec((depth, rows), lambda i: (0, i)),
            pl.BlockSpec((depth, nj * gx), lambda i: (0, 0)),
        ],
        out_specs=pl.BlockSpec((rows, nj, gx), lambda i: (i, 0, 0)),
        out_shape=jax.ShapeDtypeStruct((pts, nj, gx), jnp.float32),
        compiler_params=pltpu.CompilerParams(vmem_limit_bytes=48 << 20),
    )(flat, left, right)


def on_device(covariance, wind_x, wind_y, diffusivity, obs_point, obs_var):
    ny, gx, nj, _ = covariance.shape
    row_count, col_count = lax.axis_size("row"), lax.axis_size("col")
    row_index, col_index = lax.axis_index("row"), lax.axis_index("col")
    rows_dev, cols_dev = ny * gx, nj * gx
    sizes = (row_count, col_count, ny, gx, nj)
    obs_total = obs_point.shape[0]
    tile = covariance.reshape(rows_dev, nj, gx)

    tables = jnp.pad(
        jnp.stack(stencil_weights(wind_x, wind_y, diffusivity)), ((0, 3), (1, 1), (0, 0))
    )
    w1 = lax.dynamic_slice_in_dim(tables, row_index * ny, ny + 2, 1)
    w1 = w1.transpose(1, 2, 0).reshape((ny + 2) * gx, 8)
    w2 = lax.dynamic_slice_in_dim(tables[:5], col_index * nj, nj + 2, 1)
    w2 = w2.reshape(5 * (nj + 2), gx)

    max_row = 2 * obs_total // row_count
    max_col = 2 * obs_total // col_count
    obs_ids = jnp.arange(obs_total, dtype=jnp.int32)
    row_base, col_base = row_index * rows_dev, col_index * cols_dev

    def local(base, size, limit, other):
        start = jnp.sum((obs_point < base).astype(jnp.int32))
        padded = jnp.pad(obs_point, (0, limit), constant_values=-1)
        point = lax.dynamic_slice_in_dim(padded, start, limit, 0) - base
        return jnp.where((point >= 0) & (point < size), point, other)

    def slot_of(size):
        owner = obs_point // size
        start = jnp.sum(
            (obs_point[None, :] < (owner * size)[:, None]).astype(jnp.int32), axis=1
        )
        return owner, obs_ids - start

    row_loc = local(row_base, rows_dev, max_row, 0)
    col_loc = local(col_base, cols_dev, max_col, -1)
    row_owner, row_at = slot_of(rows_dev)
    col_owner, col_at = slot_of(cols_dev)
    row_slot = row_owner * max_row + row_at
    col_slot = col_owner * max_col + col_at

    flat, rows_part, cols_part = transport(tile, w1, w2, row_loc, col_loc[:, None], sizes)
    rows_part = rows_part.transpose(1, 0, 2).reshape(max_row, cols_dev)
    rows_all = lax.all_gather(rows_part, "row", axis=0, tiled=True)
    cols_all = lax.all_gather(cols_part, "col", axis=0, tiled=True)
    obs_rows = jnp.take(rows_all, row_slot, axis=0, mode="clip")
    obs_cols = jnp.take(cols_all, col_slot, axis=0, mode="clip")
    col_hot = (col_loc[:, None] == jnp.arange(cols_dev, dtype=jnp.int32)[None, :]).astype(
        jnp.float32
    )
    dims = (((1,), (1,)), ((), ()))
    pairs_part = lax.dot_general(col_hot, obs_rows, dims, precision=lax.Precision.HIGHEST)
    pairs_all = lax.all_gather(pairs_part, "col", axis=0, tiled=True)
    innovation = jnp.take(pairs_all, col_slot, axis=0, mode="clip").T + jnp.diag(obs_var)
    highest = lax.Precision.HIGHEST
    eye = jnp.eye(obs_total, dtype=jnp.float32)
    power = eye - innovation / newton_scale
    inverse = (eye + power) / newton_scale
    for sweep_index in range(NS_ITERS - 1):
        power = jnp.dot(power, power, precision=highest)
        inverse = inverse + jnp.dot(inverse, power, precision=highest)
    scaled = jnp.dot(inverse, obs_rows, precision=lax.Precision.HIGH)
    analysis = update(flat, obs_cols, scaled, min(256, rows_dev))
    return analysis.reshape(ny, gx, nj, gx)


def solution(mesh):
    in_specs = (P("row", None, "col", None), P(), P(), P(), P(), P())
    out_specs = P("row", None, "col", None)
    return jax.shard_map(
        on_device, mesh=mesh, in_specs=in_specs, out_specs=out_specs, check_vma=False
    )
```

```python
import functools

import jax
import jax.numpy as jnp
from jax import lax
from jax.experimental import pallas as pl
from jax.experimental.pallas import tpu as pltpu
from jax.sharding import PartitionSpec as P

STEPS = 2
NS_ITERS = 4
newton_scale = 4.0
HALO = STEPS
MESH = pl.DeviceIdType.MESH
NEAR = ((-1, 0), (1, 0), (0, -1), (0, 1), (-1, -1), (-1, 1), (1, -1), (1, 1))


def stencil_weights(wind_x, wind_y, diffusivity):
    return (
        1.0 - 4.0 * diffusivity,
        diffusivity - 0.5 * wind_x,
        diffusivity + 0.5 * wind_x,
        diffusivity - 0.5 * wind_y,
        diffusivity + 0.5 * wind_y,
    )


def split(value):
    high = value.astype(jnp.bfloat16)
    return high, (value - high.astype(jnp.float32)).astype(jnp.bfloat16)


def transport_kernel(
    sizes,
    row_ids,
    x_hbm,
    w1_ref,
    w2_ref,
    col_loc,
    flat_ref,
    rows_ref,
    cols_ref,
    ext,
    side,
    mid,
    one,
    w2b,
    local_sem,
    send_sem,
    recv_sem,
):
    row_count, col_count, ny, gx, nj = sizes
    row, col = lax.axis_index("row"), lax.axis_index("col")
    pts = ny * gx
    edge = HALO * gx
    pitch = gx + 16

    def there(dy, dx):
        return (
            (row + dy >= 0) & (row + dy < row_count) & (col + dx >= 0) & (col + dx < col_count)
        )

    load = pltpu.make_async_copy(x_hbm, ext.at[pl.ds(edge, pts)], local_sem)
    load.start()

    barrier = pltpu.get_barrier_semaphore()
    waits = 0
    for dy, dx in NEAR:
        here = there(dy, dx)

        @pl.when(here)
        def _(dy=dy, dx=dx):
            pl.semaphore_signal(
                barrier, inc=1, device_id=(row + dy, col + dx), device_id_type=MESH
            )

        waits = waits + here.astype(jnp.int32)

    def copies(slot, dy, dx):
        src_y = {-1: 0, 0: 0, 1: pts - edge}[dy]
        dst_y = {-1: edge + pts, 0: edge, 1: 0}[dy]
        length = pts if dy == 0 else edge
        target = (row + dy, col + dx)
        if dx == 0:
            pairs = [(x_hbm.at[pl.ds(src_y, length)], ext.at[pl.ds(dst_y, length)])]
        else:
            first = nj - HALO if dx > 0 else 0
            at = 0 if dx > 0 else HALO
            pairs = [
                (
                    x_hbm.at[pl.ds(src_y, length), first + k, :],
                    side.at[at + k, pl.ds(dst_y, length), :],
                )
                for k in range(HALO)
            ]
        return [
            pltpu.make_async_remote_copy(
                src_ref=src,
                dst_ref=dst,
                send_sem=send_sem.at[slot, k],
                recv_sem=recv_sem.at[slot, k],
                device_id=target,
                device_id_type=MESH,
            )
            for k, (src, dst) in enumerate(pairs)
        ]

    @pl.when(row == 0)
    def _():
        ext[pl.ds(0, edge)] = jnp.zeros((edge, nj, gx), jnp.float32)
        side[:, pl.ds(0, edge), :] = jnp.zeros((2 * HALO, edge, gx), jnp.float32)

    @pl.when(row == row_count - 1)
    def _():
        ext[pl.ds(edge + pts, edge)] = jnp.zeros((edge, nj, gx), jnp.float32)
        side[:, pl.ds(edge + pts, edge), :] = jnp.zeros((2 * HALO, edge, gx), jnp.float32)

    @pl.when(col == 0)
    def _():
        side[pl.ds(0, HALO)] = jnp.zeros((HALO, pts + 2 * edge, gx), jnp.float32)

    @pl.when(col == col_count - 1)
    def _():
        side[pl.ds(HALO, HALO)] = jnp.zeros((HALO, pts + 2 * edge, gx), jnp.float32)

    pl.semaphore_wait(barrier, waits)
    for slot, (dy, dx) in enumerate(NEAR):

        @pl.when(there(dy, dx))
        def _(slot=slot, dy=dy, dx=dx):
            for copy in copies(slot, dy, dx):
                copy.start()

    for k in range(5 * (nj + 2)):
        w2b[k] = jnp.broadcast_to(w2_ref[k : k + 1, :], (8, gx))
    load.wait()

    def arrive(slots):
        for slot in slots:
            dy, dx = NEAR[slot]

            @pl.when(there(-dy, -dx))
            def _(slot=slot, dy=dy, dx=dx):
                for copy in copies(slot, dy, dx):
                    copy.wait_recv()

    deep = 16

    def second_rows(y):
        def group(g, carry):
            at = pl.multiple_of(y * gx + g * deep, deep)
            values = [side[k, pl.ds(at, deep), :] for k in range(HALO)]
            values += [ext[pl.ds(at, deep), j, :] for j in range(nj)]
            values += [side[HALO + k, pl.ds(at, deep), :] for k in range(HALO)]
            for step in range(STEPS):
                new = []
                for j in range(1, len(values) - 1):
                    w = [
                        jnp.broadcast_to(
                            w2b[k * (nj + 2) + step + j - 1][None], (deep // 8, 8, gx)
                        ).reshape(deep, gx)
                        for k in range(5)
                    ]
                    v = values[j]
                    new.append(
                        w[0] * v
                        + w[1] * pltpu.roll(v, gx - 1, axis=1)
                        + w[2] * pltpu.roll(v, 1, axis=1)
                        + w[3] * values[j + 1]
                        + w[4] * values[j - 1]
                    )
                values = new
            to = pl.multiple_of(y * pitch + 8 + g * deep, 8)
            for j in range(nj):
                mid[j, pl.ds(to, deep), :] = values[j]
            return carry

        lax.fori_loop(0, gx // deep, group, 0, unroll=gx // deep)
        base = pl.multiple_of(y * pitch, 8)
        for j in range(nj):
            mid[j, pl.ds(base, 8), :] = mid[j, pl.ds(base + gx, 8), :]
            mid[j, pl.ds(base + 8 + gx, 8), :] = mid[j, pl.ds(base + 8, 8), :]

    def first_row(source, target, y, weight_y, to_base):
        def group(g, carry):
            at = pl.multiple_of(y * pitch + 8 + g * 8, 8)
            table = w1_ref[pl.ds(pl.multiple_of(weight_y * gx + g * 8, 8), 8), :]
            w = [jnp.broadcast_to(table[:, k : k + 1], (8, gx)) for k in range(5)]
            to = pl.multiple_of(to_base + g * 8, 8)
            for j in range(nj):
                target[j, pl.ds(to, 8), :] = (
                    w[0] * source[j, pl.ds(at, 8), :]
                    + w[1] * source[j, pl.ds(at + 1, 8), :]
                    + w[2] * source[j, pl.ds(at - 1, 8), :]
                    + w[3] * source[j, pl.ds(at + pitch, 8), :]
                    + w[4] * source[j, pl.ds(at - pitch, 8), :]
                )
            return carry

        lax.fori_loop(0, gx // 8, group, 0, unroll=gx // 8)

    def wrap(source, y):
        base = pl.multiple_of(y * pitch, 8)
        for j in range(nj):
            source[j, pl.ds(base, 8), :] = source[j, pl.ds(base + gx, 8), :]
            source[j, pl.ds(base + 8 + gx, 8), :] = source[j, pl.ds(base + 8, 8), :]

    def loop(low, high, body):
        def step(y, carry):
            body(y)
            return carry

        lax.fori_loop(low, high, step, 0)

    def one_row(y):
        first_row(mid, one, y + 1, y, y * pitch + 8)
        wrap(one, y)

    def two_row(y):
        first_row(one, flat_ref, y + 1, y + 1, y * gx)

    arrive((2, 3))
    loop(HALO, HALO + ny, second_rows)
    arrive((0, 1, 4, 5, 6, 7))
    loop(0, HALO, second_rows)
    loop(HALO + ny, 2 * HALO + ny, second_rows)
    loop(0, ny + 2, one_row)
    loop(0, ny, two_row)

    def pick(k, carry):
        at = row_ids[k]
        for j in range(nj):
            rows_ref[j, pl.ds(k, 1), :] = flat_ref[j, pl.ds(at, 1), :]
        return carry

    lax.fori_loop(0, rows_ref.shape[1], pick, 0)

    slots = cols_ref.shape[0]
    hots = []
    for j in range(nj):
        lane = lax.broadcasted_iota(jnp.int32, (slots, gx), 1) + j * gx
        hots.append((lane == col_loc[...]).astype(jnp.float32).astype(jnp.bfloat16))
    hot = jnp.concatenate(hots, axis=1)
    dims = (((1,), (1,)), ((), ()))

    def chosen(values):
        high, low = split(jnp.concatenate(values, axis=1))
        return lax.dot_general(
            hot, high, dims, preferred_element_type=jnp.float32
        ) + lax.dot_general(hot, low, dims, preferred_element_type=jnp.float32)

    half = rows_ref.shape[1] // 2
    both = chosen([rows_ref[j] for j in range(nj)])
    for side_of in range(2):
        first = side_of * (half + pts // 2)
        cols_ref[:, first : first + half] = both[:, side_of * half : (side_of + 1) * half]

    def pick_cols(y, carry):
        at = pl.multiple_of(y * gx, gx)
        to = pl.multiple_of(at + jnp.where(2 * y >= ny, 2 * half, half), gx)
        cols_ref[:, pl.ds(to, gx)] = chosen([flat_ref[j, pl.ds(at, gx), :] for j in range(nj)])
        return carry

    lax.fori_loop(0, ny, pick_cols, 0)

    for slot, (dy, dx) in enumerate(NEAR):

        @pl.when(there(dy, dx))
        def _(slot=slot, dy=dy, dx=dx):
            for copy in copies(slot, dy, dx):
                copy.wait_send()


def transport(tile, w1, w2, row_loc, col_loc, sizes):
    row_count, col_count, ny, gx, nj = sizes
    pts, edge, pitch = ny * gx, HALO * gx, gx + 16
    max_row, max_col = row_loc.shape[0], col_loc.shape[0]
    vmem = pl.BlockSpec(memory_space=pltpu.VMEM)
    return pl.pallas_call(
        functools.partial(transport_kernel, sizes),
        in_specs=[
            pl.BlockSpec(memory_space=pltpu.SMEM),
            pl.BlockSpec(memory_space=pl.ANY),
            vmem,
            vmem,
            vmem,
        ],
        out_specs=[vmem, vmem, vmem],
        out_shape=[
            jax.ShapeDtypeStruct((nj, pts, gx), jnp.float32),
            jax.ShapeDtypeStruct((nj, max_row, gx), jnp.float32),
            jax.ShapeDtypeStruct((max_col, max_row + pts), jnp.float32),
        ],
        scratch_shapes=[
            pltpu.VMEM((pts + 2 * edge, nj, gx), jnp.float32),
            pltpu.VMEM((2 * HALO, pts + 2 * edge, gx), jnp.float32),
            pltpu.VMEM((nj, (ny + 4) * pitch, gx), jnp.float32),
            pltpu.VMEM((nj, (ny + 2) * pitch, gx), jnp.float32),
            pltpu.VMEM((5 * (nj + 2), 8, gx), jnp.float32),
            pltpu.SemaphoreType.DMA(()),
            pltpu.SemaphoreType.DMA((8, HALO)),
            pltpu.SemaphoreType.DMA((8, HALO)),
        ],
        compiler_params=pltpu.CompilerParams(
            collective_id=0, has_side_effects=True, vmem_limit_bytes=62 << 20
        ),
    )(row_loc, tile, w1, w2, col_loc)


def dot3(left, right):
    l_hi, l_lo = split(left)
    r_hi, r_lo = split(right)
    return (
        jnp.dot(l_hi, r_hi, preferred_element_type=jnp.float32)
        + jnp.dot(l_hi, r_lo, preferred_element_type=jnp.float32)
        + jnp.dot(l_lo, r_hi, preferred_element_type=jnp.float32)
    )


def one_hot(mask):
    return mask.astype(jnp.float32).astype(jnp.bfloat16)


def gather_kernel(
    sizes,
    cols_in,
    rows_in,
    mine_ref,
    peer_ref,
    slot_down,
    slot_across,
    var_ref,
    f_ref,
    s_ref,
    peer,
    own,
    up_in,
    down_in,
    up_out,
    down_out,
    parts,
    pairs,
    power,
    inverse,
    wide,
    peer_sem,
    rows_sem,
    up_sem,
    down_sem,
    pair_sem,
    twin_sem,
    half_sem,
):
    row_count, col_count, ny, gx, nj = sizes
    row, col = lax.axis_index("row"), lax.axis_index("col")
    pts = ny * gx
    place, core = col // 2, lax.rem(col, 2)
    places = col_count // 2
    twin = col + 1 - 2 * core
    chunks, total = own.shape[0], own.shape[1]
    ahead = chunks - pts // 2 // gx
    width = chunks * gx
    below, above = place > 0, place < places - 1

    barrier = pltpu.get_barrier_semaphore()
    waits = row_count + below.astype(jnp.int32) + above.astype(jnp.int32)

    def greet(target):
        pl.semaphore_signal(barrier, inc=1, device_id=target, device_id_type=MESH)

    greet((row, twin))
    for hop in range(1, row_count):
        greet((lax.rem(row + hop, row_count), col))
    pl.when(below)(lambda: greet((row, col - 2)))
    pl.when(above)(lambda: greet((row, col + 2)))
    pl.semaphore_wait(barrier, waits)

    def remote(src, dst, sems, index, target):
        return pltpu.make_async_remote_copy(
            src_ref=src,
            dst_ref=dst,
            send_sem=sems.at[(0, *index)],
            recv_sem=sems.at[(1, *index)],
            device_id=target,
            device_id_type=MESH,
        )

    other = pl.multiple_of((1 - core) * width, gx)
    swap = remote(cols_in.at[:, pl.ds(other, width)], peer, peer_sem, (), (row, twin))
    swap.start()

    def rows_copy(hop):
        return remote(
            rows_in, parts.at[row], rows_sem, (hop - 1,), (lax.rem(row + hop, row_count), col)
        )

    def rows_landed(hop):
        source = lax.rem(row + row_count - hop, row_count)
        return remote(rows_in, parts.at[source], rows_sem, (hop - 1,), (source, col))

    for hop in range(1, row_count):
        rows_copy(hop).start()
    parts[row] = rows_in[...]

    ids = lax.broadcasted_iota(jnp.int32, (total, cols_in.shape[0]), 1)
    mine_hot = one_hot(ids == mine_ref[...])
    peer_hot = one_hot(ids == peer_ref[...])
    first = pl.multiple_of(core * width, gx)
    swap.wait_recv()

    def placed(hot, value):
        high, low = split(value)
        return jnp.dot(hot, high, preferred_element_type=jnp.float32) + jnp.dot(
            hot, low, preferred_element_type=jnp.float32
        )

    for chunk in range(chunks):
        at = pl.multiple_of(first + chunk * gx, gx)
        own[chunk] = placed(mine_hot, cols_in[:, pl.ds(at, gx)]) + placed(
            peer_hot, peer[:, chunk * gx : (chunk + 1) * gx]
        )

    def up_copy(chunk):
        return remote(up_out.at[chunk], up_in.at[chunk], up_sem, (chunk,), (row, col + 2))

    def down_copy(chunk):
        return remote(down_out.at[chunk], down_in.at[chunk], down_sem, (chunk,), (row, col - 2))

    def pair_copy(index, hop):
        return remote(
            pairs.at[row, core, index],
            pairs.at[row, core, index],
            pair_sem,
            (index, hop - 1),
            (lax.rem(row + hop, row_count), col),
        )

    def pair_landed(index, hop):
        source = lax.rem(row + row_count - hop, row_count)
        ref = pairs.at[source, core, index]
        return remote(ref, ref, pair_sem, (index, hop - 1), (source, col))

    def twin_copy(index, hop):
        source = lax.rem(row + row_count - hop, row_count)
        ref = pairs.at[source, core, index]
        return remote(ref, ref, twin_sem, (index, hop), (row, twin))

    def twin_landed(index, hop):
        source = lax.rem(row + row_count - hop, row_count)
        ref = pairs.at[source, 1 - core, index]
        return remote(ref, ref, twin_sem, (index, hop), (row, twin))

    def half_copy(chunk):
        ref = f_ref.at[core * (chunks - ahead) + chunk]
        return remote(ref, ref, half_sem, (chunk,), (row, twin))

    def half_landed(chunk):
        ref = f_ref.at[(1 - core) * (chunks - ahead) + chunk]
        return remote(ref, ref, half_sem, (chunk,), (row, twin))

    def forward(chunk):
        @pl.when(jnp.logical_not(below))
        def _():
            up_in[chunk] = jnp.zeros_like(up_in[chunk])

        @pl.when(below)
        def _():
            up_copy(chunk).wait_recv()

        @pl.when(above)
        def _():
            up_out[chunk] = up_in[chunk] + own[chunk]
            up_copy(chunk).start()

        @pl.when(jnp.logical_not(above))
        def _():
            down_in[chunk] = jnp.zeros_like(down_in[chunk])

        @pl.when(above)
        def _():
            down_copy(chunk).wait_recv()

        @pl.when(below)
        def _():
            down_out[chunk] = down_in[chunk] + own[chunk]
            down_copy(chunk).start()

    def finish(chunk):
        value = up_in[chunk] + own[chunk] + down_in[chunk]
        if chunk < ahead:
            pairs[row, core, chunk] = value
            for hop in range(1, row_count):
                pair_copy(chunk, hop).start()
            twin_copy(chunk, 0).start()
        else:
            f_ref[core * (chunks - ahead) + chunk - ahead] = value
            half_copy(chunk - ahead).start()

    def relay():
        for index in range(ahead):
            for hop in range(1, row_count):
                pair_landed(index, hop).wait_recv()
                twin_copy(index, hop).start()

    for chunk in range(chunks):
        forward(chunk)
        finish(chunk)
    relay()
    for index in range(ahead):
        for hop in range(row_count):
            twin_landed(index, hop).wait_recv()

    half = ahead * gx
    slots = row_count * 2 * half
    innovation = None
    for r in range(row_count):
        values = [pairs[r, q, index] for q in range(2) for index in range(ahead)]
        high, low = split(jnp.concatenate(values, axis=1))
        at = lax.broadcasted_iota(jnp.int32, (2 * half, total), 0) + r * 2 * half
        hot = one_hot(at == slot_across[...])
        term = jnp.dot(high, hot, preferred_element_type=jnp.float32) + jnp.dot(
            low, hot, preferred_element_type=jnp.float32
        )
        innovation = term if innovation is None else innovation + term
    diagonal = lax.broadcasted_iota(jnp.int32, (total, total), 0) == lax.broadcasted_iota(
        jnp.int32, (total, total), 1
    )
    eye = diagonal.astype(jnp.float32)
    innovation = innovation + jnp.where(diagonal, var_ref[...], 0.0)
    power[...] = eye - innovation / newton_scale
    inverse[...] = (eye + power[...]) / newton_scale
    for sweep_index in range(NS_ITERS - 1):
        power[...] = dot3(power[...], power[...])
        inverse[...] = inverse[...] + dot3(inverse[...], power[...])
    hot = one_hot(
        lax.broadcasted_iota(jnp.int32, (total, slots), 1) == slot_down[...]
    )
    wide[...] = placed_right(inverse[...], hot)

    for hop in range(1, row_count):
        rows_landed(hop).wait_recv()
    step = min(2, nj)
    for j in range(0, nj, step):
        right = jnp.concatenate(
            [parts[:, j + k].reshape(slots, gx) for k in range(step)], axis=1
        )
        value = dot3(wide[...], right)
        for k in range(step):
            s_ref[j + k] = value[:, k * gx : (k + 1) * gx]

    for chunk in range(chunks - ahead):
        half_landed(chunk).wait_recv()
        half_copy(chunk).wait_send()
    swap.wait_send()
    for hop in range(1, row_count):
        rows_copy(hop).wait_send()
    for index in range(ahead):
        for hop in range(1, row_count):
            pair_copy(index, hop).wait_send()
        for hop in range(row_count):
            twin_copy(index, hop).wait_send()
    for chunk in range(chunks):
        pl.when(above)(lambda: up_copy(chunk).wait_send())
        pl.when(below)(lambda: down_copy(chunk).wait_send())


def placed_right(value, hot):
    high, low = split(value)
    return jnp.dot(high, hot, preferred_element_type=jnp.float32) + jnp.dot(
        low, hot, preferred_element_type=jnp.float32
    )


def gather(cols_part, rows_part, mine, peer, slot, var, sizes):
    row_count, col_count, ny, gx, nj = sizes
    pts, total = ny * gx, var.shape[0]
    max_col, max_row = cols_part.shape[0], rows_part.shape[1]
    ahead = max_row // 2 // gx
    chunks = ahead + pts // 2 // gx
    vmem = pl.BlockSpec(memory_space=pltpu.VMEM)
    dma = pltpu.SemaphoreType.DMA
    f32 = jnp.float32
    return pl.pallas_call(
        functools.partial(gather_kernel, sizes),
        in_specs=[vmem] * 7,
        out_specs=[vmem, vmem],
        out_shape=[
            jax.ShapeDtypeStruct((pts // gx, total, gx), f32),
            jax.ShapeDtypeStruct((nj, total, gx), f32),
        ],
        scratch_shapes=[
            pltpu.VMEM((max_col, chunks * gx), f32),
            pltpu.VMEM((chunks, total, gx), f32),
            pltpu.VMEM((chunks, total, gx), f32),
            pltpu.VMEM((chunks, total, gx), f32),
            pltpu.VMEM((chunks, total, gx), f32),
            pltpu.VMEM((chunks, total, gx), f32),
            pltpu.VMEM((row_count, nj, max_row, gx), f32),
            pltpu.VMEM((row_count, 2, ahead, total, gx), f32),
            pltpu.VMEM((total, total), f32),
            pltpu.VMEM((total, total), f32),
            pltpu.VMEM((total, row_count * max_row), f32),
            dma((2,)),
            dma((2, row_count - 1)),
            dma((2, chunks)),
            dma((2, chunks)),
            dma((2, ahead, row_count - 1)),
            dma((2, ahead, row_count)),
            dma((2, chunks - ahead)),
        ],
        compiler_params=pltpu.CompilerParams(
            collective_id=1, has_side_effects=True, vmem_limit_bytes=60 << 20
        ),
    )(
        cols_part,
        rows_part,
        mine[:, None],
        peer[:, None],
        slot[:, None],
        slot[None, :],
        var[None, :],
    )


def update_kernel(nj, gx, rows, flat_ref, left_ref, right_ref, out_ref):
    left = jnp.concatenate([left_ref[k].T for k in range(left_ref.shape[0])], axis=0)
    l_hi, l_lo = split(left)
    wide = min(2, nj)
    for j in range(0, nj, wide):
        r_hi, r_lo = split(
            jnp.concatenate([right_ref[j + k] for k in range(wide)], axis=1)
        )
        total = (
            jnp.dot(l_hi, r_hi, preferred_element_type=jnp.float32)
            + jnp.dot(l_hi, r_lo, preferred_element_type=jnp.float32)
            + jnp.dot(l_lo, r_hi, preferred_element_type=jnp.float32)
        )
        for k in range(wide):
            out_ref[:, j + k, :] = flat_ref[j + k] - total[:, k * gx : (k + 1) * gx]


def update(flat, left, right, rows):
    nj, pts, gx = flat.shape
    depth = left.shape[1]
    return pl.pallas_call(
        functools.partial(update_kernel, nj, gx, rows),
        grid=(pts // rows,),
        in_specs=[
            pl.BlockSpec((nj, rows, gx), lambda i: (0, i, 0)),
            pl.BlockSpec((rows // gx, depth, gx), lambda i: (i, 0, 0)),
            pl.BlockSpec((nj, depth, gx), lambda i: (0, 0, 0)),
        ],
        out_specs=pl.BlockSpec((rows, nj, gx), lambda i: (i, 0, 0)),
        out_shape=jax.ShapeDtypeStruct((pts, nj, gx), jnp.float32),
        compiler_params=pltpu.CompilerParams(vmem_limit_bytes=48 << 20),
    )(flat, left, right)


def on_device(covariance, wind_x, wind_y, diffusivity, obs_point, obs_var):
    ny, gx, nj, _ = covariance.shape
    row_count, col_count = lax.axis_size("row"), lax.axis_size("col")
    row_index, col_index = lax.axis_index("row"), lax.axis_index("col")
    rows_dev, cols_dev = ny * gx, nj * gx
    sizes = (row_count, col_count, ny, gx, nj)
    obs_total = obs_point.shape[0]
    tile = covariance.reshape(rows_dev, nj, gx)

    tables = jnp.pad(
        jnp.stack(stencil_weights(wind_x, wind_y, diffusivity)), ((0, 3), (1, 1), (0, 0))
    )
    w1 = lax.dynamic_slice_in_dim(tables, row_index * ny, ny + 2, 1)
    w1 = w1.transpose(1, 2, 0).reshape((ny + 2) * gx, 8)
    w2 = lax.dynamic_slice_in_dim(tables[:5], col_index * nj, nj + 2, 1)
    w2 = w2.reshape(5 * (nj + 2), gx)

    max_row = max(2 * gx, 2 * obs_total // row_count)
    max_col = max(gx, 2 * obs_total // col_count)
    obs_ids = jnp.arange(obs_total, dtype=jnp.int32)
    row_base, col_base = row_index * rows_dev, col_index * cols_dev

    def local(base, size, limit, other):
        start = jnp.sum((obs_point < base).astype(jnp.int32))
        padded = jnp.pad(obs_point, (0, limit), constant_values=-1)
        point = lax.dynamic_slice_in_dim(padded, start, limit, 0) - base
        return jnp.where((point >= 0) & (point < size), point, other)

    def slot_of(size):
        owner = obs_point // size
        start = jnp.sum(
            (obs_point[None, :] < (owner * size)[:, None]).astype(jnp.int32), axis=1
        )
        return owner, obs_ids - start

    row_loc = local(row_base, rows_dev, max_row, 0)
    col_loc = local(col_base, cols_dev, max_col, -1)
    row_owner, row_at = slot_of(rows_dev)
    col_owner, col_at = slot_of(cols_dev)
    row_slot = row_owner * max_row + row_at

    flat, rows_part, cols_part = transport(tile, w1, w2, row_loc, col_loc[:, None], sizes)
    mine = jnp.where(col_owner == col_index, col_at, -1)
    peer = jnp.where(col_owner == col_index + 1 - 2 * (col_index % 2), col_at, -1)
    columns, scaled = gather(cols_part, rows_part, mine, peer, row_slot, obs_var, sizes)
    analysis = update(flat, columns, scaled, min(256, rows_dev))
    return analysis.reshape(ny, gx, nj, gx)


def solution(mesh):
    in_specs = (P("row", None, "col", None), P(), P(), P(), P(), P())
    out_specs = P("row", None, "col", None)
    return jax.shard_map(
        on_device, mesh=mesh, in_specs=in_specs, out_specs=out_specs, check_vma=False
    )
```

```python
import functools

import jax
import jax.numpy as jnp
from jax import lax
from jax.experimental import pallas as pl
from jax.experimental.pallas import tpu as pltpu
from jax.sharding import PartitionSpec as P

STEPS = 2
NS_ITERS = 4
newton_scale = 4.0
HALO = STEPS
LAG = 2
MESH = pl.DeviceIdType.MESH
NEAR = ((-1, 0), (1, 0), (0, -1), (0, 1), (-1, -1), (-1, 1), (1, -1), (1, 1))


def stencil_weights(wind_x, wind_y, diffusivity):
    return (
        1.0 - 4.0 * diffusivity,
        diffusivity - 0.5 * wind_x,
        diffusivity + 0.5 * wind_x,
        diffusivity - 0.5 * wind_y,
        diffusivity + 0.5 * wind_y,
    )


def split(value):
    high = value.astype(jnp.bfloat16)
    return high, (value - high.astype(jnp.float32)).astype(jnp.bfloat16)


def transport_kernel(
    sizes,
    row_ids,
    x_hbm,
    w1_ref,
    w2_ref,
    col_loc,
    flat_ref,
    rows_ref,
    cols_ref,
    ext,
    side,
    mid,
    one,
    w2b,
    local_sem,
    send_sem,
    recv_sem,
):
    row_count, col_count, ny, gx, nj = sizes
    row, col = lax.axis_index("row"), lax.axis_index("col")
    pts = ny * gx
    edge = HALO * gx
    pitch = gx + 16

    def there(dy, dx):
        return (
            (row + dy >= 0) & (row + dy < row_count) & (col + dx >= 0) & (col + dx < col_count)
        )

    load = pltpu.make_async_copy(x_hbm, ext.at[pl.ds(edge, pts)], local_sem)
    load.start()

    barrier = pltpu.get_barrier_semaphore()
    waits = 0
    for dy, dx in NEAR:
        here = there(dy, dx)

        @pl.when(here)
        def _(dy=dy, dx=dx):
            pl.semaphore_signal(
                barrier, inc=1, device_id=(row + dy, col + dx), device_id_type=MESH
            )

        waits = waits + here.astype(jnp.int32)

    def copies(slot, dy, dx):
        src_y = {-1: 0, 0: 0, 1: pts - edge}[dy]
        dst_y = {-1: edge + pts, 0: edge, 1: 0}[dy]
        length = pts if dy == 0 else edge
        target = (row + dy, col + dx)
        if dx == 0:
            pairs = [(x_hbm.at[pl.ds(src_y, length)], ext.at[pl.ds(dst_y, length)])]
        else:
            first = nj - HALO if dx > 0 else 0
            at = 0 if dx > 0 else HALO
            pairs = [
                (
                    x_hbm.at[pl.ds(src_y, length), first + k, :],
                    side.at[at + k, pl.ds(dst_y, length), :],
                )
                for k in range(HALO)
            ]
        return [
            pltpu.make_async_remote_copy(
                src_ref=src,
                dst_ref=dst,
                send_sem=send_sem.at[slot, k],
                recv_sem=recv_sem.at[slot, k],
                device_id=target,
                device_id_type=MESH,
            )
            for k, (src, dst) in enumerate(pairs)
        ]

    @pl.when(row == 0)
    def _():
        ext[pl.ds(0, edge)] = jnp.zeros((edge, nj, gx), jnp.float32)
        side[:, pl.ds(0, edge), :] = jnp.zeros((2 * HALO, edge, gx), jnp.float32)

    @pl.when(row == row_count - 1)
    def _():
        ext[pl.ds(edge + pts, edge)] = jnp.zeros((edge, nj, gx), jnp.float32)
        side[:, pl.ds(edge + pts, edge), :] = jnp.zeros((2 * HALO, edge, gx), jnp.float32)

    @pl.when(col == 0)
    def _():
        side[pl.ds(0, HALO)] = jnp.zeros((HALO, pts + 2 * edge, gx), jnp.float32)

    @pl.when(col == col_count - 1)
    def _():
        side[pl.ds(HALO, HALO)] = jnp.zeros((HALO, pts + 2 * edge, gx), jnp.float32)

    pl.semaphore_wait(barrier, waits)
    for slot, (dy, dx) in enumerate(NEAR):

        @pl.when(there(dy, dx))
        def _(slot=slot, dy=dy, dx=dx):
            for copy in copies(slot, dy, dx):
                copy.start()

    for k in range(5 * (nj + 2)):
        w2b[k] = jnp.broadcast_to(w2_ref[k : k + 1, :], (8, gx))
    load.wait()

    def arrive(slots):
        for slot in slots:
            dy, dx = NEAR[slot]

            @pl.when(there(-dy, -dx))
            def _(slot=slot, dy=dy, dx=dx):
                for copy in copies(slot, dy, dx):
                    copy.wait_recv()

    deep = 16

    def second_rows(y):
        def group(g, carry):
            at = pl.multiple_of(y * gx + g * deep, deep)
            values = [side[k, pl.ds(at, deep), :] for k in range(HALO)]
            values += [ext[pl.ds(at, deep), j, :] for j in range(nj)]
            values += [side[HALO + k, pl.ds(at, deep), :] for k in range(HALO)]
            for step in range(STEPS):
                new = []
                for j in range(1, len(values) - 1):
                    w = [
                        jnp.broadcast_to(
                            w2b[k * (nj + 2) + step + j - 1][None], (deep // 8, 8, gx)
                        ).reshape(deep, gx)
                        for k in range(5)
                    ]
                    v = values[j]
                    new.append(
                        w[0] * v
                        + w[1] * pltpu.roll(v, gx - 1, axis=1)
                        + w[2] * pltpu.roll(v, 1, axis=1)
                        + w[3] * values[j + 1]
                        + w[4] * values[j - 1]
                    )
                values = new
            to = pl.multiple_of(y * pitch + 8 + g * deep, 8)
            for j in range(nj):
                mid[j, pl.ds(to, deep), :] = values[j]
            return carry

        lax.fori_loop(0, gx // deep, group, 0, unroll=gx // deep)
        base = pl.multiple_of(y * pitch, 8)
        for j in range(nj):
            mid[j, pl.ds(base, 8), :] = mid[j, pl.ds(base + gx, 8), :]
            mid[j, pl.ds(base + 8 + gx, 8), :] = mid[j, pl.ds(base + 8, 8), :]

    def first_row(source, target, y, weight_y, to_base):
        def group(g, carry):
            at = pl.multiple_of(y * pitch + 8 + g * 8, 8)
            table = w1_ref[pl.ds(pl.multiple_of(weight_y * gx + g * 8, 8), 8), :]
            w = [jnp.broadcast_to(table[:, k : k + 1], (8, gx)) for k in range(5)]
            to = pl.multiple_of(to_base + g * 8, 8)
            for j in range(nj):
                target[j, pl.ds(to, 8), :] = (
                    w[0] * source[j, pl.ds(at, 8), :]
                    + w[1] * source[j, pl.ds(at + 1, 8), :]
                    + w[2] * source[j, pl.ds(at - 1, 8), :]
                    + w[3] * source[j, pl.ds(at + pitch, 8), :]
                    + w[4] * source[j, pl.ds(at - pitch, 8), :]
                )
            return carry

        lax.fori_loop(0, gx // 8, group, 0, unroll=gx // 8)

    def wrap(source, y):
        base = pl.multiple_of(y * pitch, 8)
        for j in range(nj):
            source[j, pl.ds(base, 8), :] = source[j, pl.ds(base + gx, 8), :]
            source[j, pl.ds(base + 8 + gx, 8), :] = source[j, pl.ds(base + 8, 8), :]

    def loop(low, high, body):
        def step(y, carry):
            body(y)
            return carry

        lax.fori_loop(low, high, step, 0)

    def one_row(y):
        first_row(mid, one, y + 1, y, y * pitch + 8)
        wrap(one, y)

    def two_row(y):
        first_row(one, flat_ref, y + 1, y + 1, y * gx)

    arrive((2, 3))
    loop(HALO, HALO + ny, second_rows)
    arrive((0, 1, 4, 5, 6, 7))
    loop(0, HALO, second_rows)
    loop(HALO + ny, 2 * HALO + ny, second_rows)
    loop(0, ny + 2, one_row)
    loop(0, ny, two_row)

    def pick(k, carry):
        at = row_ids[k]
        for j in range(nj):
            rows_ref[j, pl.ds(k, 1), :] = flat_ref[j, pl.ds(at, 1), :]
        return carry

    lax.fori_loop(0, rows_ref.shape[1], pick, 0)

    slots = cols_ref.shape[0]
    hots = []
    for j in range(nj):
        lane = lax.broadcasted_iota(jnp.int32, (slots, gx), 1) + j * gx
        hots.append((lane == col_loc[...]).astype(jnp.float32).astype(jnp.bfloat16))
    hot = jnp.concatenate(hots, axis=1)
    dims = (((1,), (1,)), ((), ()))

    def chosen(values):
        high, low = split(jnp.concatenate(values, axis=1))
        return lax.dot_general(
            hot, high, dims, preferred_element_type=jnp.float32
        ) + lax.dot_general(hot, low, dims, preferred_element_type=jnp.float32)

    half = rows_ref.shape[1] // 2
    both = chosen([rows_ref[j] for j in range(nj)])
    for side_of in range(2):
        first = side_of * (half + pts // 2)
        cols_ref[:, first : first + half] = both[:, side_of * half : (side_of + 1) * half]

    def pick_cols(y, carry):
        at = pl.multiple_of(y * gx, gx)
        to = pl.multiple_of(at + jnp.where(2 * y >= ny, 2 * half, half), gx)
        cols_ref[:, pl.ds(to, gx)] = chosen([flat_ref[j, pl.ds(at, gx), :] for j in range(nj)])
        return carry

    lax.fori_loop(0, ny, pick_cols, 0)

    for slot, (dy, dx) in enumerate(NEAR):

        @pl.when(there(dy, dx))
        def _(slot=slot, dy=dy, dx=dx):
            for copy in copies(slot, dy, dx):
                copy.wait_send()


def transport(tile, w1, w2, row_loc, col_loc, sizes):
    row_count, col_count, ny, gx, nj = sizes
    pts, edge, pitch = ny * gx, HALO * gx, gx + 16
    max_row, max_col = row_loc.shape[0], col_loc.shape[0]
    vmem = pl.BlockSpec(memory_space=pltpu.VMEM)
    return pl.pallas_call(
        functools.partial(transport_kernel, sizes),
        in_specs=[
            pl.BlockSpec(memory_space=pltpu.SMEM),
            pl.BlockSpec(memory_space=pl.ANY),
            vmem,
            vmem,
            vmem,
        ],
        out_specs=[vmem, vmem, vmem],
        out_shape=[
            jax.ShapeDtypeStruct((nj, pts, gx), jnp.float32),
            jax.ShapeDtypeStruct((nj, max_row, gx), jnp.float32),
            jax.ShapeDtypeStruct((max_col, max_row + pts), jnp.float32),
        ],
        scratch_shapes=[
            pltpu.VMEM((pts + 2 * edge, nj, gx), jnp.float32),
            pltpu.VMEM((2 * HALO, pts + 2 * edge, gx), jnp.float32),
            pltpu.VMEM((nj, (ny + 4) * pitch, gx), jnp.float32),
            pltpu.VMEM((nj, (ny + 2) * pitch, gx), jnp.float32),
            pltpu.VMEM((5 * (nj + 2), 8, gx), jnp.float32),
            pltpu.SemaphoreType.DMA(()),
            pltpu.SemaphoreType.DMA((8, HALO)),
            pltpu.SemaphoreType.DMA((8, HALO)),
        ],
        compiler_params=pltpu.CompilerParams(
            collective_id=0, has_side_effects=True, vmem_limit_bytes=62 << 20
        ),
    )(row_loc, tile, w1, w2, col_loc)


def dot3(left, right):
    l_hi, l_lo = split(left)
    r_hi, r_lo = split(right)
    return (
        jnp.dot(l_hi, r_hi, preferred_element_type=jnp.float32)
        + jnp.dot(l_hi, r_lo, preferred_element_type=jnp.float32)
        + jnp.dot(l_lo, r_hi, preferred_element_type=jnp.float32)
    )


def one_hot(mask):
    return mask.astype(jnp.float32).astype(jnp.bfloat16)


def gather_kernel(
    sizes,
    cols_in,
    rows_in,
    mine_ref,
    peer_ref,
    slot_down,
    slot_across,
    var_ref,
    f_ref,
    s_ref,
    peer,
    own,
    up_in,
    down_in,
    up_out,
    down_out,
    parts,
    pairs,
    power,
    inverse,
    wide,
    peer_sem,
    rows_sem,
    up_sem,
    down_sem,
    pair_sem,
    twin_sem,
    half_sem,
):
    row_count, col_count, ny, gx, nj = sizes
    row, col = lax.axis_index("row"), lax.axis_index("col")
    pts = ny * gx
    place, core = col // 2, lax.rem(col, 2)
    places = col_count // 2
    twin = col + 1 - 2 * core
    chunks, total = own.shape[0], 2 * own.shape[1]
    ahead = chunks - pts // gx
    width = chunks // 2 * gx
    below, above = place > 0, place < places - 1

    barrier = pltpu.get_barrier_semaphore()
    waits = row_count + below.astype(jnp.int32) + above.astype(jnp.int32)

    def greet(target):
        pl.semaphore_signal(barrier, inc=1, device_id=target, device_id_type=MESH)

    greet((row, twin))
    for hop in range(1, row_count):
        greet((lax.rem(row + hop, row_count), col))
    pl.when(below)(lambda: greet((row, col - 2)))
    pl.when(above)(lambda: greet((row, col + 2)))
    pl.semaphore_wait(barrier, waits)

    def remote(src, dst, sems, index, target):
        return pltpu.make_async_remote_copy(
            src_ref=src,
            dst_ref=dst,
            send_sem=sems.at[(0, *index)],
            recv_sem=sems.at[(1, *index)],
            device_id=target,
            device_id_type=MESH,
        )

    other = pl.multiple_of((1 - core) * width, gx)
    swap = remote(cols_in.at[:, pl.ds(other, width)], peer, peer_sem, (), (row, twin))
    swap.start()

    def rows_copy(hop):
        return remote(
            rows_in, parts.at[row], rows_sem, (hop - 1,), (lax.rem(row + hop, row_count), col)
        )

    def rows_landed(hop):
        source = lax.rem(row + row_count - hop, row_count)
        return remote(rows_in, parts.at[source], rows_sem, (hop - 1,), (source, col))

    for hop in range(1, row_count):
        rows_copy(hop).start()
    parts[row] = rows_in[...]

    ids = lax.broadcasted_iota(jnp.int32, (total, cols_in.shape[0]), 1)
    mine_hot = one_hot(ids == mine_ref[...])
    peer_hot = one_hot(ids == peer_ref[...])
    first = pl.multiple_of(core * width, gx)
    swap.wait_recv()

    def placed(hot, value):
        high, low = split(value)
        return jnp.dot(hot, high, preferred_element_type=jnp.float32) + jnp.dot(
            hot, low, preferred_element_type=jnp.float32
        )

    for piece in range(chunks // 2):
        at = pl.multiple_of(first + piece * gx, gx)
        value = placed(mine_hot, cols_in[:, pl.ds(at, gx)]) + placed(
            peer_hot, peer[:, piece * gx : (piece + 1) * gx]
        )
        own[2 * piece] = value[: total // 2]
        own[2 * piece + 1] = value[total // 2 :]

    @pl.when(jnp.logical_not(below))
    def _():
        up_in[...] = jnp.zeros_like(up_in)

    @pl.when(jnp.logical_not(above))
    def _():
        down_in[...] = jnp.zeros_like(down_in)

    def up_copy(chunk):
        return remote(up_out.at[chunk], up_in.at[chunk], up_sem, (chunk,), (row, col + 2))

    def down_copy(chunk):
        return remote(down_out.at[chunk], down_in.at[chunk], down_sem, (chunk,), (row, col - 2))

    def pair_copy(index, hop):
        return remote(
            pairs.at[row, core, index],
            pairs.at[row, core, index],
            pair_sem,
            (index, hop - 1),
            (lax.rem(row + hop, row_count), col),
        )

    def pair_landed(index, hop):
        source = lax.rem(row + row_count - hop, row_count)
        ref = pairs.at[source, core, index]
        return remote(ref, ref, pair_sem, (index, hop - 1), (source, col))

    def twin_copy(index, hop):
        source = lax.rem(row + row_count - hop, row_count)
        ref = pairs.at[source, core, index]
        return remote(ref, ref, twin_sem, (index, hop), (row, twin))

    def twin_landed(index, hop):
        source = lax.rem(row + row_count - hop, row_count)
        ref = pairs.at[source, 1 - core, index]
        return remote(ref, ref, twin_sem, (index, hop), (row, twin))

    def half_copy(chunk):
        ref = f_ref.at[core * (chunks - ahead) + chunk]
        return remote(ref, ref, half_sem, (chunk,), (row, twin))

    def half_landed(chunk):
        ref = f_ref.at[(1 - core) * (chunks - ahead) + chunk]
        return remote(ref, ref, half_sem, (chunk,), (row, twin))

    def up_stage(chunk):
        @pl.when(below)
        def _():
            up_copy(chunk).wait_recv()

        @pl.when(above)
        def _():
            up_out[chunk] = up_in[chunk] + own[chunk]
            up_copy(chunk).start()

    def down_stage(chunk):
        @pl.when(above)
        def _():
            down_copy(chunk).wait_recv()

        @pl.when(below)
        def _():
            down_out[chunk] = down_in[chunk] + own[chunk]
            down_copy(chunk).start()

    def finish(chunk):
        value = up_in[chunk] + own[chunk] + down_in[chunk]

        @pl.when(chunk < ahead)
        def _():
            pairs[row, core, chunk] = value
            for hop in range(1, row_count):
                pair_copy(chunk, hop).start()
            twin_copy(chunk, 0).start()

        @pl.when(chunk >= ahead)
        def _():
            f_ref[core * (chunks - ahead) + chunk - ahead] = value
            half_copy(chunk - ahead).start()

    def relay():
        for index in range(ahead):
            for hop in range(1, row_count):
                pair_landed(index, hop).wait_recv()
                twin_copy(index, hop).start()

    from_below, from_above = LAG * place, LAG * (places - 1 - place)
    for tick in range(chunks + LAG * (places - 1)):
        for stage, lag in (
            (up_stage, from_below),
            (down_stage, from_above),
            (finish, jnp.maximum(from_below, from_above)),
        ):
            chunk = tick - lag

            @pl.when((chunk >= 0) & (chunk < chunks))
            def _(stage=stage, chunk=chunk):
                stage(chunk)

    relay()
    for index in range(ahead):
        for hop in range(row_count):
            twin_landed(index, hop).wait_recv()

    half = ahead // 2 * gx
    slots = row_count * 2 * half
    innovation = None
    for r in range(row_count):
        values = [
            jnp.concatenate([pairs[r, q, 2 * k], pairs[r, q, 2 * k + 1]], axis=0)
            for q in range(2)
            for k in range(ahead // 2)
        ]
        high, low = split(jnp.concatenate(values, axis=1))
        at = lax.broadcasted_iota(jnp.int32, (2 * half, total), 0) + r * 2 * half
        hot = one_hot(at == slot_across[...])
        term = jnp.dot(high, hot, preferred_element_type=jnp.float32) + jnp.dot(
            low, hot, preferred_element_type=jnp.float32
        )
        innovation = term if innovation is None else innovation + term
    diagonal = lax.broadcasted_iota(jnp.int32, (total, total), 0) == lax.broadcasted_iota(
        jnp.int32, (total, total), 1
    )
    eye = diagonal.astype(jnp.float32)
    innovation = innovation + jnp.where(diagonal, var_ref[...], 0.0)
    power[...] = eye - innovation / newton_scale
    inverse[...] = (eye + power[...]) / newton_scale
    for sweep_index in range(NS_ITERS - 1):
        power[...] = dot3(power[...], power[...])
        inverse[...] = inverse[...] + dot3(inverse[...], power[...])
    hot = one_hot(
        lax.broadcasted_iota(jnp.int32, (total, slots), 1) == slot_down[...]
    )
    wide[...] = placed_right(inverse[...], hot)

    for hop in range(1, row_count):
        rows_landed(hop).wait_recv()
    step = min(2, nj)
    for j in range(0, nj, step):
        right = jnp.concatenate(
            [parts[:, j + k].reshape(slots, gx) for k in range(step)], axis=1
        )
        value = dot3(wide[...], right)
        for k in range(step):
            s_ref[j + k] = value[:, k * gx : (k + 1) * gx]

    for chunk in range(chunks - ahead):
        half_landed(chunk).wait_recv()
        half_copy(chunk).wait_send()
    swap.wait_send()
    for hop in range(1, row_count):
        rows_copy(hop).wait_send()
    for index in range(ahead):
        for hop in range(1, row_count):
            pair_copy(index, hop).wait_send()
        for hop in range(row_count):
            twin_copy(index, hop).wait_send()
    for chunk in range(chunks):
        pl.when(above)(lambda: up_copy(chunk).wait_send())
        pl.when(below)(lambda: down_copy(chunk).wait_send())


def placed_right(value, hot):
    high, low = split(value)
    return jnp.dot(high, hot, preferred_element_type=jnp.float32) + jnp.dot(
        low, hot, preferred_element_type=jnp.float32
    )


def gather(cols_part, rows_part, mine, peer, slot, var, sizes):
    row_count, col_count, ny, gx, nj = sizes
    pts, total = ny * gx, var.shape[0]
    max_col, max_row = cols_part.shape[0], rows_part.shape[1]
    ahead = max_row // gx
    chunks = ahead + pts // gx
    vmem = pl.BlockSpec(memory_space=pltpu.VMEM)
    dma = pltpu.SemaphoreType.DMA
    f32 = jnp.float32
    return pl.pallas_call(
        functools.partial(gather_kernel, sizes),
        in_specs=[vmem] * 7,
        out_specs=[vmem, vmem],
        out_shape=[
            jax.ShapeDtypeStruct((2 * pts // gx, total // 2, gx), f32),
            jax.ShapeDtypeStruct((nj, total, gx), f32),
        ],
        scratch_shapes=[
            pltpu.VMEM((max_col, chunks // 2 * gx), f32),
            pltpu.VMEM((chunks, total // 2, gx), f32),
            pltpu.VMEM((chunks, total // 2, gx), f32),
            pltpu.VMEM((chunks, total // 2, gx), f32),
            pltpu.VMEM((chunks, total // 2, gx), f32),
            pltpu.VMEM((chunks, total // 2, gx), f32),
            pltpu.VMEM((row_count, nj, max_row, gx), f32),
            pltpu.VMEM((row_count, 2, ahead, total // 2, gx), f32),
            pltpu.VMEM((total, total), f32),
            pltpu.VMEM((total, total), f32),
            pltpu.VMEM((total, row_count * max_row), f32),
            dma((2,)),
            dma((2, row_count - 1)),
            dma((2, chunks)),
            dma((2, chunks)),
            dma((2, ahead, row_count - 1)),
            dma((2, ahead, row_count)),
            dma((2, chunks - ahead)),
        ],
        compiler_params=pltpu.CompilerParams(
            collective_id=1, has_side_effects=True, vmem_limit_bytes=60 << 20
        ),
    )(
        cols_part,
        rows_part,
        mine[:, None],
        peer[:, None],
        slot[:, None],
        slot[None, :],
        var[None, :],
    )


def update_kernel(nj, gx, rows, flat_ref, left_ref, right_ref, out_ref):
    left = jnp.concatenate([left_ref[k].T for k in range(left_ref.shape[0])], axis=0)
    l_hi, l_lo = split(left)
    wide = min(2, nj)
    for j in range(0, nj, wide):
        r_hi, r_lo = split(
            jnp.concatenate([right_ref[j + k] for k in range(wide)], axis=1)
        )
        total = (
            jnp.dot(l_hi, r_hi, preferred_element_type=jnp.float32)
            + jnp.dot(l_hi, r_lo, preferred_element_type=jnp.float32)
            + jnp.dot(l_lo, r_hi, preferred_element_type=jnp.float32)
        )
        for k in range(wide):
            out_ref[:, j + k, :] = flat_ref[j + k] - total[:, k * gx : (k + 1) * gx]


def update(flat, left, right, rows):
    nj, pts, gx = flat.shape
    depth = left.shape[1]
    return pl.pallas_call(
        functools.partial(update_kernel, nj, gx, rows),
        grid=(pts // rows,),
        in_specs=[
            pl.BlockSpec((nj, rows, gx), lambda i: (0, i, 0)),
            pl.BlockSpec((rows // gx, depth, gx), lambda i: (i, 0, 0)),
            pl.BlockSpec((nj, depth, gx), lambda i: (0, 0, 0)),
        ],
        out_specs=pl.BlockSpec((rows, nj, gx), lambda i: (i, 0, 0)),
        out_shape=jax.ShapeDtypeStruct((pts, nj, gx), jnp.float32),
        compiler_params=pltpu.CompilerParams(vmem_limit_bytes=48 << 20),
    )(flat, left, right)


def on_device(covariance, wind_x, wind_y, diffusivity, obs_point, obs_var):
    ny, gx, nj, _ = covariance.shape
    row_count, col_count = lax.axis_size("row"), lax.axis_size("col")
    row_index, col_index = lax.axis_index("row"), lax.axis_index("col")
    rows_dev, cols_dev = ny * gx, nj * gx
    sizes = (row_count, col_count, ny, gx, nj)
    obs_total = obs_point.shape[0]
    tile = covariance.reshape(rows_dev, nj, gx)

    tables = jnp.pad(
        jnp.stack(stencil_weights(wind_x, wind_y, diffusivity)), ((0, 3), (1, 1), (0, 0))
    )
    w1 = lax.dynamic_slice_in_dim(tables, row_index * ny, ny + 2, 1)
    w1 = w1.transpose(1, 2, 0).reshape((ny + 2) * gx, 8)
    w2 = lax.dynamic_slice_in_dim(tables[:5], col_index * nj, nj + 2, 1)
    w2 = w2.reshape(5 * (nj + 2), gx)

    max_row = max(2 * gx, 2 * obs_total // row_count)
    max_col = max(gx, 2 * obs_total // col_count)
    obs_ids = jnp.arange(obs_total, dtype=jnp.int32)
    row_base, col_base = row_index * rows_dev, col_index * cols_dev

    def local(base, size, limit, other):
        start = jnp.sum((obs_point < base).astype(jnp.int32))
        padded = jnp.pad(obs_point, (0, limit), constant_values=-1)
        point = lax.dynamic_slice_in_dim(padded, start, limit, 0) - base
        return jnp.where((point >= 0) & (point < size), point, other)

    def slot_of(size):
        owner = obs_point // size
        start = jnp.sum(
            (obs_point[None, :] < (owner * size)[:, None]).astype(jnp.int32), axis=1
        )
        return owner, obs_ids - start

    row_loc = local(row_base, rows_dev, max_row, 0)
    col_loc = local(col_base, cols_dev, max_col, -1)
    row_owner, row_at = slot_of(rows_dev)
    col_owner, col_at = slot_of(cols_dev)
    row_slot = row_owner * max_row + row_at

    flat, rows_part, cols_part = transport(tile, w1, w2, row_loc, col_loc[:, None], sizes)
    mine = jnp.where(col_owner == col_index, col_at, -1)
    peer = jnp.where(col_owner == col_index + 1 - 2 * (col_index % 2), col_at, -1)
    columns, scaled = gather(cols_part, rows_part, mine, peer, row_slot, obs_var, sizes)
    columns = columns.reshape(rows_dev // gx, obs_total, gx)
    analysis = update(flat, columns, scaled, min(256, rows_dev))
    return analysis.reshape(ny, gx, nj, gx)


def solution(mesh):
    in_specs = (P("row", None, "col", None), P(), P(), P(), P(), P())
    out_specs = P("row", None, "col", None)
    return jax.shard_map(
        on_device, mesh=mesh, in_specs=in_specs, out_specs=out_specs, check_vma=False
    )
```

```python
import functools

import jax
import jax.numpy as jnp
from jax import lax
from jax.experimental import pallas as pl
from jax.experimental.pallas import tpu as pltpu
from jax.sharding import PartitionSpec as P

STEPS = 2
NS_ITERS = 4
newton_scale = 4.0
HALO = STEPS
LAG = 2
FIRST_WORK = 17
MESH = pl.DeviceIdType.MESH


def stencil_weights(wind_x, wind_y, diffusivity):
    return (
        1.0 - 4.0 * diffusivity,
        diffusivity - 0.5 * wind_x,
        diffusivity + 0.5 * wind_x,
        diffusivity - 0.5 * wind_y,
        diffusivity + 0.5 * wind_y,
    )


def split(value):
    high = value.astype(jnp.bfloat16)
    return high, (value - high.astype(jnp.float32)).astype(jnp.bfloat16)


def transport_kernel(
    sizes,
    obs_ref,
    x_hbm,
    wind_x,
    wind_y,
    diffusivity,
    flat_ref,
    rows_ref,
    cols_ref,
    ext,
    side,
    mid,
    one,
    tables,
    w1_ref,
    w2b,
    col_loc,
    local_sem,
    row_sem,
    col_sem,
    corner_sem,
):
    row_count, col_count, ny, gx, nj = sizes
    row, col = lax.axis_index("row"), lax.axis_index("col")
    pts = ny * gx
    edge = HALO * gx
    pitch = gx + 16
    bottom = edge + pts

    load = pltpu.make_async_copy(x_hbm, ext.at[pl.ds(edge, pts)], local_sem)
    load.start()

    north, south, west, east = row > 0, row < row_count - 1, col > 0, col < col_count - 1
    barrier = pltpu.get_barrier_semaphore()
    waits = 0
    for here, target in (
        (north, (row - 1, col)),
        (south, (row + 1, col)),
        (west, (row, col - 1)),
        (east, (row, col + 1)),
    ):

        @pl.when(here)
        def _(target=target):
            pl.semaphore_signal(barrier, inc=1, device_id=target, device_id_type=MESH)

        waits = waits + here.astype(jnp.int32)

    def remote(src, dst, sems, index, target):
        return pltpu.make_async_remote_copy(
            src_ref=src,
            dst_ref=dst,
            send_sem=sems.at[(0, *index)],
            recv_sem=sems.at[(1, *index)],
            device_id=target,
            device_id_type=MESH,
        )

    pieces = ((0, nj),) if nj < 2 * HALO + 1 else ((0, HALO), (nj - HALO, HALO), (HALO, nj - 2 * HALO))
    urgent = min(2, len(pieces))

    def row_copy(way, piece):
        at, size = pieces[piece]
        src_y, dst_y, to = ((0, bottom, row - 1), (pts - edge, 0, row + 1))[way]
        return remote(
            x_hbm.at[pl.ds(src_y, edge), pl.ds(at, size), :],
            ext.at[pl.ds(dst_y, edge), pl.ds(at, size), :],
            row_sem,
            (way, piece),
            (to, col),
        )

    def col_copy(way, k):
        src_j, dst_j, to = ((k, HALO + k, col - 1), (nj - HALO + k, k, col + 1))[way]
        return remote(
            x_hbm.at[:, src_j, :],
            side.at[dst_j, pl.ds(edge, pts), :],
            col_sem,
            (way, k),
            (row, to),
        )

    def corner_copy(way, part, k):
        src_j, dst_j, to = ((k, HALO + k, col - 1), (nj - HALO + k, k, col + 1))[way]
        at = (0, bottom)[part]
        return remote(
            ext.at[pl.ds(at, edge), src_j, :],
            side.at[dst_j, pl.ds(at, edge), :],
            corner_sem,
            (way, part, k),
            (row, to),
        )

    row_to, row_from = (north, south), (south, north)
    col_to, col_from = (west, east), (east, west)
    parts = (north, south)

    @pl.when(jnp.logical_not(north))
    def _():
        ext[pl.ds(0, edge)] = jnp.zeros((edge, nj, gx), jnp.float32)
        side[:, pl.ds(0, edge), :] = jnp.zeros((2 * HALO, edge, gx), jnp.float32)

    @pl.when(jnp.logical_not(south))
    def _():
        ext[pl.ds(bottom, edge)] = jnp.zeros((edge, nj, gx), jnp.float32)
        side[:, pl.ds(bottom, edge), :] = jnp.zeros((2 * HALO, edge, gx), jnp.float32)

    @pl.when(jnp.logical_not(west))
    def _():
        side[pl.ds(0, HALO)] = jnp.zeros((HALO, pts + 2 * edge, gx), jnp.float32)

    @pl.when(jnp.logical_not(east))
    def _():
        side[pl.ds(HALO, HALO)] = jnp.zeros((HALO, pts + 2 * edge, gx), jnp.float32)

    pl.semaphore_wait(barrier, waits)

    def each(here, copies, act):
        @pl.when(here)
        def _():
            for copy in copies():
                act(copy)

    start = lambda copy: copy.start()
    landed = lambda copy: copy.wait_recv()
    sent = lambda copy: copy.wait_send()

    def rows(flags, which, act):
        for way in range(2):
            each(flags[way], lambda: [row_copy(way, piece) for piece in which], act)

    def columns(flags, act):
        for way in range(2):
            each(flags[way], lambda: [col_copy(way, k) for k in range(HALO)], act)

    def corners(flags, act):
        for way in range(2):
            for part in range(2):
                each(
                    flags[way] & parts[part],
                    lambda: [corner_copy(way, part, k) for k in range(HALO)],
                    act,
                )

    all_pieces = range(len(pieces))
    rows(row_to, all_pieces[:urgent], start)
    columns(col_to, start)
    rows(row_to, all_pieces[urgent:], start)

    grid_y = wind_x.shape[0]
    tables[pl.ds(0, 8)] = jnp.zeros((8, gx), jnp.float32)
    tables[pl.ds((grid_y + 1) * 8, 8)] = jnp.zeros((8, gx), jnp.float32)
    weights = stencil_weights(wind_x[...], wind_y[...], diffusivity[...])
    for k in range(8):
        value = weights[k] if k < 5 else jnp.zeros((grid_y, gx), jnp.float32)
        tables[pl.ds(8 + k, grid_y, stride=8), :] = value
    for j in range(nj + 2):
        block = tables[pl.ds(pl.multiple_of((col * nj + j) * 8, 8), 8), :]
        for k in range(5):
            w2b[k * (nj + 2) + j] = jnp.broadcast_to(block[k : k + 1], (8, gx))
    for y in range(ny + 2):
        block = tables[pl.ds(pl.multiple_of((row * ny + y) * 8, 8), 8), :]
        w1_ref[y * gx : (y + 1) * gx, :] = jnp.concatenate(
            [block, jnp.zeros((gx - 8, gx), jnp.float32)], axis=0
        ).T

    obs_total = obs_ref.shape[0]
    cols_dev = nj * gx

    def count(k, carry):
        point = obs_ref[k]
        return (
            carry[0] + (point < row * pts).astype(jnp.int32),
            carry[1] + (point < col * cols_dev).astype(jnp.int32),
        )

    zero = jnp.int32(0)
    row_start, col_start = lax.fori_loop(0, obs_total, count, (zero, zero), unroll=8)

    def place_column(k, carry):
        at = col_start + k
        point = obs_ref[jnp.minimum(at, obs_total - 1)] - col * cols_dev
        point = jnp.where(at < obs_total, point, -1)
        col_loc[pl.ds(k, 1), :] = jnp.full((1, gx), point, jnp.int32)
        return carry

    lax.fori_loop(0, col_loc.shape[0], place_column, 0)
    load.wait()

    deep = 16

    def second_rows(y):
        def group(g, carry):
            at = pl.multiple_of(y * gx + g * deep, deep)
            values = [side[k, pl.ds(at, deep), :] for k in range(HALO)]
            values += [ext[pl.ds(at, deep), j, :] for j in range(nj)]
            values += [side[HALO + k, pl.ds(at, deep), :] for k in range(HALO)]
            for step in range(STEPS):
                new = []
                for j in range(1, len(values) - 1):
                    w = [
                        jnp.broadcast_to(
                            w2b[k * (nj + 2) + step + j - 1][None], (deep // 8, 8, gx)
                        ).reshape(deep, gx)
                        for k in range(5)
                    ]
                    v = values[j]
                    new.append(
                        w[0] * v
                        + w[1] * pltpu.roll(v, gx - 1, axis=1)
                        + w[2] * pltpu.roll(v, 1, axis=1)
                        + w[3] * values[j + 1]
                        + w[4] * values[j - 1]
                    )
                values = new
            to = pl.multiple_of(y * pitch + 8 + g * deep, 8)
            for j in range(nj):
                mid[j, pl.ds(to, deep), :] = values[j]
            return carry

        lax.fori_loop(0, gx // deep, group, 0, unroll=gx // deep)
        base = pl.multiple_of(y * pitch, 8)
        for j in range(nj):
            mid[j, pl.ds(base, 8), :] = mid[j, pl.ds(base + gx, 8), :]
            mid[j, pl.ds(base + 8 + gx, 8), :] = mid[j, pl.ds(base + 8, 8), :]

    def first_row(source, target, y, weight_y, to_base):
        def group(g, carry):
            at = pl.multiple_of(y * pitch + 8 + g * 8, 8)
            table = w1_ref[pl.ds(pl.multiple_of(weight_y * gx + g * 8, 8), 8), :]
            w = [jnp.broadcast_to(table[:, k : k + 1], (8, gx)) for k in range(5)]
            to = pl.multiple_of(to_base + g * 8, 8)
            for j in range(nj):
                target[j, pl.ds(to, 8), :] = (
                    w[0] * source[j, pl.ds(at, 8), :]
                    + w[1] * source[j, pl.ds(at + 1, 8), :]
                    + w[2] * source[j, pl.ds(at - 1, 8), :]
                    + w[3] * source[j, pl.ds(at + pitch, 8), :]
                    + w[4] * source[j, pl.ds(at - pitch, 8), :]
                )
            return carry

        lax.fori_loop(0, gx // 8, group, 0, unroll=gx // 8)

    def wrap(source, y):
        base = pl.multiple_of(y * pitch, 8)
        for j in range(nj):
            source[j, pl.ds(base, 8), :] = source[j, pl.ds(base + gx, 8), :]
            source[j, pl.ds(base + 8 + gx, 8), :] = source[j, pl.ds(base + 8, 8), :]

    def loop(low, high, body):
        def step(y, carry):
            body(y)
            return carry

        lax.fori_loop(low, high, step, 0)

    def one_row(y):
        first_row(mid, one, y + 1, y, y * pitch + 8)
        wrap(one, y)

    def two_row(y):
        first_row(one, flat_ref, y + 1, y + 1, y * gx)

    rows(row_from, all_pieces[:urgent], landed)
    corners(col_to, start)
    columns(col_from, landed)
    low, high = min(HALO, ny // 2), max(ny - HALO, ny // 2)
    loop(HALO, HALO + ny, second_rows)
    loop(2, ny, one_row)
    loop(low, high, two_row)
    rows(row_from, all_pieces[urgent:], landed)
    corners(col_from, landed)
    loop(0, HALO, second_rows)
    loop(HALO + ny, 2 * HALO + ny, second_rows)
    loop(0, 2, one_row)
    loop(ny, ny + 2, one_row)
    loop(0, low, two_row)
    loop(high, ny, two_row)

    def pick(k, carry):
        at = obs_ref[jnp.minimum(row_start + k, obs_total - 1)] - row * pts
        at = jnp.clip(at, 0, pts - 1)
        for j in range(nj):
            rows_ref[j, pl.ds(k, 1), :] = flat_ref[j, pl.ds(at, 1), :]
        return carry

    lax.fori_loop(0, rows_ref.shape[1], pick, 0)

    slots = cols_ref.shape[0]
    hots = []
    for j in range(nj):
        lane = lax.broadcasted_iota(jnp.int32, (slots, gx), 1) + j * gx
        hots.append((lane == col_loc[...]).astype(jnp.float32).astype(jnp.bfloat16))
    hot = jnp.concatenate(hots, axis=1)
    dims = (((1,), (1,)), ((), ()))

    def chosen(values):
        high, low = split(jnp.concatenate(values, axis=1))
        return lax.dot_general(
            hot, high, dims, preferred_element_type=jnp.float32
        ) + lax.dot_general(hot, low, dims, preferred_element_type=jnp.float32)

    half = rows_ref.shape[1] // 2
    both = chosen([rows_ref[j] for j in range(nj)])
    for side_of in range(2):
        first = side_of * (half + pts // 2)
        cols_ref[:, first : first + half] = both[:, side_of * half : (side_of + 1) * half]

    def pick_cols(y, carry):
        at = pl.multiple_of(y * gx, gx)
        to = pl.multiple_of(at + jnp.where(2 * y >= ny, 2 * half, half), gx)
        cols_ref[:, pl.ds(to, gx)] = chosen([flat_ref[j, pl.ds(at, gx), :] for j in range(nj)])
        return carry

    lax.fori_loop(0, ny, pick_cols, 0)

    rows(row_to, all_pieces, sent)
    columns(col_to, sent)
    corners(col_to, sent)


def transport(tile, obs_point, winds, max_row, max_col, sizes):
    row_count, col_count, ny, gx, nj = sizes
    pts, edge, pitch = ny * gx, HALO * gx, gx + 16
    grid_y = winds[0].shape[0]
    vmem = pl.BlockSpec(memory_space=pltpu.VMEM)
    return pl.pallas_call(
        functools.partial(transport_kernel, sizes),
        in_specs=[
            pl.BlockSpec(memory_space=pltpu.SMEM),
            pl.BlockSpec(memory_space=pl.ANY),
            vmem,
            vmem,
            vmem,
        ],
        out_specs=[vmem, vmem, vmem],
        out_shape=[
            jax.ShapeDtypeStruct((nj, pts, gx), jnp.float32),
            jax.ShapeDtypeStruct((nj, max_row, gx), jnp.float32),
            jax.ShapeDtypeStruct((max_col, max_row + pts), jnp.float32),
        ],
        scratch_shapes=[
            pltpu.VMEM((pts + 2 * edge, nj, gx), jnp.float32),
            pltpu.VMEM((2 * HALO, pts + 2 * edge, gx), jnp.float32),
            pltpu.VMEM((nj, (ny + 4) * pitch, gx), jnp.float32),
            pltpu.VMEM((nj, (ny + 2) * pitch, gx), jnp.float32),
            pltpu.VMEM(((grid_y + 2) * 8, gx), jnp.float32),
            pltpu.VMEM(((ny + 2) * gx, gx), jnp.float32),
            pltpu.VMEM((5 * (nj + 2), 8, gx), jnp.float32),
            pltpu.VMEM((max_col, gx), jnp.int32),
            pltpu.SemaphoreType.DMA(()),
            pltpu.SemaphoreType.DMA((2, 2, 3)),
            pltpu.SemaphoreType.DMA((2, 2, HALO)),
            pltpu.SemaphoreType.DMA((2, 2, 2, HALO)),
        ],
        compiler_params=pltpu.CompilerParams(
            collective_id=0, has_side_effects=True, vmem_limit_bytes=62 << 20
        ),
    )(obs_point, tile, *winds)


def dot3(left, right):
    l_hi, l_lo = split(left)
    r_hi, r_lo = split(right)
    return (
        jnp.dot(l_hi, r_hi, preferred_element_type=jnp.float32)
        + jnp.dot(l_hi, r_lo, preferred_element_type=jnp.float32)
        + jnp.dot(l_lo, r_hi, preferred_element_type=jnp.float32)
    )


def one_hot(mask):
    return mask.astype(jnp.float32).astype(jnp.bfloat16)


def gather_kernel(
    sizes,
    cols_in,
    rows_in,
    obs_ref,
    var_ref,
    f_ref,
    s_ref,
    peer,
    own,
    up_in,
    down_in,
    up_out,
    down_out,
    parts,
    pairs,
    power,
    inverse,
    wide,
    peer_sem,
    rows_sem,
    up_sem,
    down_sem,
    pair_sem,
    twin_sem,
    half_sem,
):
    row_count, col_count, ny, gx, nj = sizes
    row, col = lax.axis_index("row"), lax.axis_index("col")
    pts = ny * gx
    place, core = col // 2, lax.rem(col, 2)
    places = col_count // 2
    twin = col + 1 - 2 * core
    chunks, total = own.shape[0], 2 * own.shape[1]
    ahead = chunks - pts // gx
    width = chunks // 2 * gx
    below, above = place > 0, place < places - 1

    barrier = pltpu.get_barrier_semaphore()
    waits = row_count + below.astype(jnp.int32) + above.astype(jnp.int32)

    def greet(target):
        pl.semaphore_signal(barrier, inc=1, device_id=target, device_id_type=MESH)

    greet((row, twin))
    for hop in range(1, row_count):
        greet((lax.rem(row + hop, row_count), col))
    pl.when(below)(lambda: greet((row, col - 2)))
    pl.when(above)(lambda: greet((row, col + 2)))
    pl.semaphore_wait(barrier, waits)

    def remote(src, dst, sems, index, target):
        return pltpu.make_async_remote_copy(
            src_ref=src,
            dst_ref=dst,
            send_sem=sems.at[(0, *index)],
            recv_sem=sems.at[(1, *index)],
            device_id=target,
            device_id_type=MESH,
        )

    other = pl.multiple_of((1 - core) * width, gx)
    swap = remote(cols_in.at[:, pl.ds(other, width)], peer, peer_sem, (), (row, twin))
    swap.start()

    def rows_copy(hop):
        return remote(
            rows_in, parts.at[row], rows_sem, (hop - 1,), (lax.rem(row + hop, row_count), col)
        )

    def rows_landed(hop):
        source = lax.rem(row + row_count - hop, row_count)
        return remote(rows_in, parts.at[source], rows_sem, (hop - 1,), (source, col))

    for hop in range(1, row_count):
        rows_copy(hop).start()
    parts[row] = rows_in[...]

    points = obs_ref[...]
    ids = lax.broadcasted_iota(jnp.int32, (1, total), 1).astype(jnp.float32)

    def before(limit):
        return jnp.sum((points < limit).astype(jnp.float32), axis=1, keepdims=True)

    def within(block):
        size = nj * gx
        here = (points >= block * size) & (points < (block + 1) * size)
        return jnp.where(here, ids - before(block * size), -1.0)

    slot_across = ids
    max_row = rows_in.shape[1]
    for r in range(1, row_count):
        fewer = before(r * pts) - before((r - 1) * pts)
        slot_across = slot_across + jnp.where(points >= r * pts, max_row - fewer, 0.0)
    stack = jnp.concatenate(
        [within(col), within(twin), slot_across, jnp.zeros((gx - 3, total), jnp.float32)], axis=0
    ).T
    slot_down = stack[:, 2:3]
    lanes = lax.broadcasted_iota(jnp.int32, (total, cols_in.shape[0]), 1).astype(jnp.float32)
    mine_hot = one_hot(lanes == stack[:, 0:1])
    peer_hot = one_hot(lanes == stack[:, 1:2])
    first = pl.multiple_of(core * width, gx)
    swap.wait_recv()

    def placed(hot, value):
        high, low = split(value)
        return jnp.dot(hot, high, preferred_element_type=jnp.float32) + jnp.dot(
            hot, low, preferred_element_type=jnp.float32
        )

    for piece in range(chunks // 2):
        at = pl.multiple_of(first + piece * gx, gx)
        value = placed(mine_hot, cols_in[:, pl.ds(at, gx)]) + placed(
            peer_hot, peer[:, piece * gx : (piece + 1) * gx]
        )
        own[2 * piece] = value[: total // 2]
        own[2 * piece + 1] = value[total // 2 :]

    @pl.when(jnp.logical_not(below))
    def _():
        up_in[...] = jnp.zeros_like(up_in)

    @pl.when(jnp.logical_not(above))
    def _():
        down_in[...] = jnp.zeros_like(down_in)

    def up_copy(chunk):
        return remote(up_out.at[chunk], up_in.at[chunk], up_sem, (chunk,), (row, col + 2))

    def down_copy(chunk):
        return remote(down_out.at[chunk], down_in.at[chunk], down_sem, (chunk,), (row, col - 2))

    def pair_copy(index, hop):
        return remote(
            pairs.at[row, core, index],
            pairs.at[row, core, index],
            pair_sem,
            (index, hop - 1),
            (lax.rem(row + hop, row_count), col),
        )

    def pair_landed(index, hop):
        source = lax.rem(row + row_count - hop, row_count)
        ref = pairs.at[source, core, index]
        return remote(ref, ref, pair_sem, (index, hop - 1), (source, col))

    def twin_copy(index, hop):
        source = lax.rem(row + row_count - hop, row_count)
        ref = pairs.at[source, core, index]
        return remote(ref, ref, twin_sem, (index, hop), (row, twin))

    def twin_landed(index, hop):
        source = lax.rem(row + row_count - hop, row_count)
        ref = pairs.at[source, 1 - core, index]
        return remote(ref, ref, twin_sem, (index, hop), (row, twin))

    def half_copy(chunk):
        ref = f_ref.at[core * (chunks - ahead) + chunk]
        return remote(ref, ref, half_sem, (chunk,), (row, twin))

    def half_landed(chunk):
        ref = f_ref.at[(1 - core) * (chunks - ahead) + chunk]
        return remote(ref, ref, half_sem, (chunk,), (row, twin))

    def up_stage(chunk):
        @pl.when(below)
        def _():
            up_copy(chunk).wait_recv()

        @pl.when(above)
        def _():
            up_out[chunk] = up_in[chunk] + own[chunk]
            up_copy(chunk).start()

    def down_stage(chunk):
        @pl.when(above)
        def _():
            down_copy(chunk).wait_recv()

        @pl.when(below)
        def _():
            down_out[chunk] = down_in[chunk] + own[chunk]
            down_copy(chunk).start()

    def finish(chunk):
        value = up_in[chunk] + own[chunk] + down_in[chunk]

        @pl.when(chunk < ahead)
        def _():
            pairs[row, core, chunk] = value
            for hop in range(1, row_count):
                pair_copy(chunk, hop).start()
            twin_copy(chunk, 0).start()

        @pl.when(chunk >= ahead)
        def _():
            f_ref[core * (chunks - ahead) + chunk - ahead] = value
            half_copy(chunk - ahead).start()

    def relay():
        for index in range(ahead):
            for hop in range(1, row_count):
                pair_landed(index, hop).wait_recv()
                twin_copy(index, hop).start()

    half = ahead // 2 * gx
    slots = row_count * 2 * half

    def twins():
        for index in range(ahead):
            for hop in range(row_count):
                twin_landed(index, hop).wait_recv()

    def gathered():
        innovation = None
        for r in range(row_count):
            values = [
                jnp.concatenate([pairs[r, q, 2 * k], pairs[r, q, 2 * k + 1]], axis=0)
                for q in range(2)
                for k in range(ahead // 2)
            ]
            high, low = split(jnp.concatenate(values, axis=1))
            at = lax.broadcasted_iota(jnp.int32, (2 * half, total), 0) + r * 2 * half
            hot = one_hot(at.astype(jnp.float32) == slot_across)
            term = jnp.dot(high, hot, preferred_element_type=jnp.float32) + jnp.dot(
                low, hot, preferred_element_type=jnp.float32
            )
            innovation = term if innovation is None else innovation + term
        diagonal = lax.broadcasted_iota(jnp.int32, (total, total), 0) == lax.broadcasted_iota(
            jnp.int32, (total, total), 1
        )
        eye = diagonal.astype(jnp.float32)
        innovation = innovation + jnp.where(diagonal, var_ref[...], 0.0)
        power[...] = eye - innovation / newton_scale
        inverse[...] = (eye + power[...]) / newton_scale

    def square():
        power[...] = dot3(power[...], power[...])

    def sweep():
        inverse[...] = inverse[...] + dot3(inverse[...], power[...])

    def widen():
        at = lax.broadcasted_iota(jnp.int32, (total, slots), 1).astype(jnp.float32)
        wide[...] = placed_right(inverse[...], one_hot(at == slot_down))

    work = [relay, twins, gathered] + [square, sweep] * (NS_ITERS - 1) + [widen]

    from_below, from_above = LAG * place, LAG * (places - 1 - place)
    for tick in range(chunks + LAG * (places - 1)):
        for stage, lag in (
            (up_stage, from_below),
            (down_stage, from_above),
            (finish, jnp.maximum(from_below, from_above)),
        ):
            chunk = tick - lag

            @pl.when((chunk >= 0) & (chunk < chunks))
            def _(stage=stage, chunk=chunk):
                stage(chunk)

        if tick >= FIRST_WORK and work:
            work.pop(0)()
    for task in work:
        task()
    for hop in range(1, row_count):
        rows_landed(hop).wait_recv()
    step = min(2, nj)
    for j in range(0, nj, step):
        right = jnp.concatenate(
            [parts[:, j + k].reshape(slots, gx) for k in range(step)], axis=1
        )
        value = dot3(wide[...], right)
        for k in range(step):
            s_ref[j + k] = value[:, k * gx : (k + 1) * gx]

    for chunk in range(chunks - ahead):
        half_landed(chunk).wait_recv()
        half_copy(chunk).wait_send()
    swap.wait_send()
    for hop in range(1, row_count):
        rows_copy(hop).wait_send()
    for index in range(ahead):
        for hop in range(1, row_count):
            pair_copy(index, hop).wait_send()
        for hop in range(row_count):
            twin_copy(index, hop).wait_send()
    for chunk in range(chunks):
        pl.when(above)(lambda: up_copy(chunk).wait_send())
        pl.when(below)(lambda: down_copy(chunk).wait_send())


def placed_right(value, hot):
    high, low = split(value)
    return jnp.dot(high, hot, preferred_element_type=jnp.float32) + jnp.dot(
        low, hot, preferred_element_type=jnp.float32
    )


def gather(cols_part, rows_part, obs_point, var, sizes):
    row_count, col_count, ny, gx, nj = sizes
    pts, total = ny * gx, var.shape[0]
    max_col, max_row = cols_part.shape[0], rows_part.shape[1]
    ahead = max_row // gx
    chunks = ahead + pts // gx
    vmem = pl.BlockSpec(memory_space=pltpu.VMEM)
    dma = pltpu.SemaphoreType.DMA
    f32 = jnp.float32
    return pl.pallas_call(
        functools.partial(gather_kernel, sizes),
        in_specs=[vmem] * 4,
        out_specs=[vmem, vmem],
        out_shape=[
            jax.ShapeDtypeStruct((2 * pts // gx, total // 2, gx), f32),
            jax.ShapeDtypeStruct((nj, total, gx), f32),
        ],
        scratch_shapes=[
            pltpu.VMEM((max_col, chunks // 2 * gx), f32),
            pltpu.VMEM((chunks, total // 2, gx), f32),
            pltpu.VMEM((chunks, total // 2, gx), f32),
            pltpu.VMEM((chunks, total // 2, gx), f32),
            pltpu.VMEM((chunks, total // 2, gx), f32),
            pltpu.VMEM((chunks, total // 2, gx), f32),
            pltpu.VMEM((row_count, nj, max_row, gx), f32),
            pltpu.VMEM((row_count, 2, ahead, total // 2, gx), f32),
            pltpu.VMEM((total, total), f32),
            pltpu.VMEM((total, total), f32),
            pltpu.VMEM((total, row_count * max_row), f32),
            dma((2,)),
            dma((2, row_count - 1)),
            dma((2, chunks)),
            dma((2, chunks)),
            dma((2, ahead, row_count - 1)),
            dma((2, ahead, row_count)),
            dma((2, chunks - ahead)),
        ],
        compiler_params=pltpu.CompilerParams(
            collective_id=1, has_side_effects=True, vmem_limit_bytes=60 << 20
        ),
    )(cols_part, rows_part, obs_point[None, :], var[None, :])


def update_kernel(nj, gx, rows, flat_ref, left_ref, right_ref, out_ref):
    left = jnp.concatenate([left_ref[k].T for k in range(left_ref.shape[0])], axis=0)
    l_hi, l_lo = split(left)
    wide = min(2, nj)
    for j in range(0, nj, wide):
        r_hi, r_lo = split(
            jnp.concatenate([right_ref[j + k] for k in range(wide)], axis=1)
        )
        total = (
            jnp.dot(l_hi, r_hi, preferred_element_type=jnp.float32)
            + jnp.dot(l_hi, r_lo, preferred_element_type=jnp.float32)
            + jnp.dot(l_lo, r_hi, preferred_element_type=jnp.float32)
        )
        for k in range(wide):
            out_ref[:, j + k, :] = flat_ref[j + k] - total[:, k * gx : (k + 1) * gx]


def update(flat, left, right, rows):
    nj, pts, gx = flat.shape
    depth = left.shape[1]
    return pl.pallas_call(
        functools.partial(update_kernel, nj, gx, rows),
        grid=(pts // rows,),
        in_specs=[
            pl.BlockSpec((nj, rows, gx), lambda i: (0, i, 0)),
            pl.BlockSpec((rows // gx, depth, gx), lambda i: (i, 0, 0)),
            pl.BlockSpec((nj, depth, gx), lambda i: (0, 0, 0)),
        ],
        out_specs=pl.BlockSpec((rows, nj, gx), lambda i: (i, 0, 0)),
        out_shape=jax.ShapeDtypeStruct((pts, nj, gx), jnp.float32),
        compiler_params=pltpu.CompilerParams(vmem_limit_bytes=48 << 20),
    )(flat, left, right)


def on_device(covariance, wind_x, wind_y, diffusivity, obs_point, obs_var):
    ny, gx, nj, _ = covariance.shape
    row_count, col_count = lax.axis_size("row"), lax.axis_size("col")
    rows_dev = ny * gx
    sizes = (row_count, col_count, ny, gx, nj)
    obs_total = obs_point.shape[0]
    tile = covariance.reshape(rows_dev, nj, gx)

    max_row = max(2 * gx, 2 * obs_total // row_count)
    max_col = max(gx, 2 * obs_total // col_count)
    winds = (wind_x, wind_y, diffusivity)
    flat, rows_part, cols_part = transport(tile, obs_point, winds, max_row, max_col, sizes)
    columns, scaled = gather(cols_part, rows_part, obs_point, obs_var, sizes)
    columns = columns.reshape(rows_dev // gx, obs_total, gx)
    analysis = update(flat, columns, scaled, min(256, rows_dev))
    return analysis.reshape(ny, gx, nj, gx)


def solution(mesh):
    in_specs = (P("row", None, "col", None), P(), P(), P(), P(), P())
    out_specs = P("row", None, "col", None)
    return jax.shard_map(
        on_device, mesh=mesh, in_specs=in_specs, out_specs=out_specs, check_vma=False
    )
```

```python
import functools

import jax
import jax.numpy as jnp
from jax import lax
from jax.experimental import pallas as pl
from jax.experimental.pallas import tpu as pltpu
from jax.sharding import PartitionSpec as P

STEPS = 2
NS_ITERS = 4
newton_scale = 4.0
HALO = STEPS
LAG = 2
FIRST_WORK = 20
MESH = pl.DeviceIdType.MESH


def stencil_weights(wind_x, wind_y, diffusivity):
    return (
        1.0 - 4.0 * diffusivity,
        diffusivity - 0.5 * wind_x,
        diffusivity + 0.5 * wind_x,
        diffusivity - 0.5 * wind_y,
        diffusivity + 0.5 * wind_y,
    )


def split(value):
    high = value.astype(jnp.bfloat16)
    return high, (value - high.astype(jnp.float32)).astype(jnp.bfloat16)


def transport_kernel(
    sizes,
    obs_ref,
    x_hbm,
    wind_x,
    wind_y,
    diffusivity,
    flat_ref,
    rows_ref,
    cols_ref,
    ext,
    side,
    mid,
    one,
    tables,
    w1_ref,
    w2b,
    col_loc,
    local_sem,
    row_sem,
    col_sem,
    corner_sem,
):
    row_count, col_count, ny, gx, nj = sizes
    row, col = lax.axis_index("row"), lax.axis_index("col")
    pts = ny * gx
    edge = HALO * gx
    pitch = gx + 16
    bottom = edge + pts

    load = pltpu.make_async_copy(x_hbm, ext.at[pl.ds(edge, pts)], local_sem)
    load.start()

    north, south, west, east = row > 0, row < row_count - 1, col > 0, col < col_count - 1
    barrier = pltpu.get_barrier_semaphore()
    waits = 0
    for here, target in (
        (north, (row - 1, col)),
        (south, (row + 1, col)),
        (west, (row, col - 1)),
        (east, (row, col + 1)),
    ):

        @pl.when(here)
        def _(target=target):
            pl.semaphore_signal(barrier, inc=1, device_id=target, device_id_type=MESH)

        waits = waits + here.astype(jnp.int32)

    def remote(src, dst, sems, index, target):
        return pltpu.make_async_remote_copy(
            src_ref=src,
            dst_ref=dst,
            send_sem=sems.at[(0, *index)],
            recv_sem=sems.at[(1, *index)],
            device_id=target,
            device_id_type=MESH,
        )

    pieces = ((0, nj),) if nj < 2 * HALO + 1 else ((0, HALO), (nj - HALO, HALO), (HALO, nj - 2 * HALO))
    urgent = min(2, len(pieces))

    def row_copy(way, piece):
        at, size = pieces[piece]
        src_y, dst_y, to = ((0, bottom, row - 1), (pts - edge, 0, row + 1))[way]
        return remote(
            x_hbm.at[pl.ds(src_y, edge), pl.ds(at, size), :],
            ext.at[pl.ds(dst_y, edge), pl.ds(at, size), :],
            row_sem,
            (way, piece),
            (to, col),
        )

    def col_copy(way, k):
        src_j, dst_j, to = ((k, HALO + k, col - 1), (nj - HALO + k, k, col + 1))[way]
        return remote(
            x_hbm.at[:, src_j, :],
            side.at[dst_j, pl.ds(edge, pts), :],
            col_sem,
            (way, k),
            (row, to),
        )

    def corner_copy(way, part, k):
        src_j, dst_j, to = ((k, HALO + k, col - 1), (nj - HALO + k, k, col + 1))[way]
        at = (0, bottom)[part]
        return remote(
            ext.at[pl.ds(at, edge), src_j, :],
            side.at[dst_j, pl.ds(at, edge), :],
            corner_sem,
            (way, part, k),
            (row, to),
        )

    row_to, row_from = (north, south), (south, north)
    col_to, col_from = (west, east), (east, west)
    parts = (north, south)

    @pl.when(jnp.logical_not(north))
    def _():
        ext[pl.ds(0, edge)] = jnp.zeros((edge, nj, gx), jnp.float32)
        side[:, pl.ds(0, edge), :] = jnp.zeros((2 * HALO, edge, gx), jnp.float32)

    @pl.when(jnp.logical_not(south))
    def _():
        ext[pl.ds(bottom, edge)] = jnp.zeros((edge, nj, gx), jnp.float32)
        side[:, pl.ds(bottom, edge), :] = jnp.zeros((2 * HALO, edge, gx), jnp.float32)

    @pl.when(jnp.logical_not(west))
    def _():
        side[pl.ds(0, HALO)] = jnp.zeros((HALO, pts + 2 * edge, gx), jnp.float32)

    @pl.when(jnp.logical_not(east))
    def _():
        side[pl.ds(HALO, HALO)] = jnp.zeros((HALO, pts + 2 * edge, gx), jnp.float32)

    pl.semaphore_wait(barrier, waits)

    def each(here, copies, act):
        @pl.when(here)
        def _():
            for copy in copies():
                act(copy)

    start = lambda copy: copy.start()
    landed = lambda copy: copy.wait_recv()
    sent = lambda copy: copy.wait_send()

    def rows(flags, which, act):
        for way in range(2):
            each(flags[way], lambda: [row_copy(way, piece) for piece in which], act)

    def columns(flags, act):
        for way in range(2):
            each(flags[way], lambda: [col_copy(way, k) for k in range(HALO)], act)

    def corners(flags, act):
        for way in range(2):
            for part in range(2):
                each(
                    flags[way] & parts[part],
                    lambda: [corner_copy(way, part, k) for k in range(HALO)],
                    act,
                )

    all_pieces = range(len(pieces))
    rows(row_to, all_pieces[:urgent], start)
    columns(col_to, start)
    rows(row_to, all_pieces[urgent:], start)

    grid_y = wind_x.shape[0]
    tables[pl.ds(0, 8)] = jnp.zeros((8, gx), jnp.float32)
    tables[pl.ds((grid_y + 1) * 8, 8)] = jnp.zeros((8, gx), jnp.float32)
    weights = stencil_weights(wind_x[...], wind_y[...], diffusivity[...])
    for k in range(8):
        value = weights[k] if k < 5 else jnp.zeros((grid_y, gx), jnp.float32)
        tables[pl.ds(8 + k, grid_y, stride=8), :] = value
    for j in range(nj + 2):
        block = tables[pl.ds(pl.multiple_of((col * nj + j) * 8, 8), 8), :]
        for k in range(5):
            w2b[k * (nj + 2) + j] = jnp.broadcast_to(block[k : k + 1], (8, gx))
    for y in range(ny + 2):
        block = tables[pl.ds(pl.multiple_of((row * ny + y) * 8, 8), 8), :]
        w1_ref[y * gx : (y + 1) * gx, :] = jnp.concatenate(
            [block, jnp.zeros((gx - 8, gx), jnp.float32)], axis=0
        ).T

    obs_total = obs_ref.shape[0]
    cols_dev = nj * gx

    def count(k, carry):
        point = obs_ref[k]
        return (
            carry[0] + (point < row * pts).astype(jnp.int32),
            carry[1] + (point < col * cols_dev).astype(jnp.int32),
        )

    zero = jnp.int32(0)
    row_start, col_start = lax.fori_loop(0, obs_total, count, (zero, zero), unroll=8)

    def place_column(k, carry):
        at = col_start + k
        point = obs_ref[jnp.minimum(at, obs_total - 1)] - col * cols_dev
        point = jnp.where(at < obs_total, point, -1)
        col_loc[pl.ds(k, 1), :] = jnp.full((1, gx), point, jnp.int32)
        return carry

    lax.fori_loop(0, col_loc.shape[0], place_column, 0)
    load.wait()

    deep = 16

    def second_rows(y):
        def group(g, carry):
            at = pl.multiple_of(y * gx + g * deep, deep)
            values = [side[k, pl.ds(at, deep), :] for k in range(HALO)]
            values += [ext[pl.ds(at, deep), j, :] for j in range(nj)]
            values += [side[HALO + k, pl.ds(at, deep), :] for k in range(HALO)]
            for step in range(STEPS):
                new = []
                for j in range(1, len(values) - 1):
                    w = [
                        jnp.broadcast_to(
                            w2b[k * (nj + 2) + step + j - 1][None], (deep // 8, 8, gx)
                        ).reshape(deep, gx)
                        for k in range(5)
                    ]
                    v = values[j]
                    new.append(
                        w[0] * v
                        + w[1] * pltpu.roll(v, gx - 1, axis=1)
                        + w[2] * pltpu.roll(v, 1, axis=1)
                        + w[3] * values[j + 1]
                        + w[4] * values[j - 1]
                    )
                values = new
            to = pl.multiple_of(y * pitch + 8 + g * deep, 8)
            for j in range(nj):
                mid[j, pl.ds(to, deep), :] = values[j]
            return carry

        lax.fori_loop(0, gx // deep, group, 0, unroll=gx // deep)
        base = pl.multiple_of(y * pitch, 8)
        for j in range(nj):
            mid[j, pl.ds(base, 8), :] = mid[j, pl.ds(base + gx, 8), :]
            mid[j, pl.ds(base + 8 + gx, 8), :] = mid[j, pl.ds(base + 8, 8), :]

    def first_row(source, target, y, weight_y, to_base):
        def group(g, carry):
            at = pl.multiple_of(y * pitch + 8 + g * 8, 8)
            table = w1_ref[pl.ds(pl.multiple_of(weight_y * gx + g * 8, 8), 8), :]
            w = [jnp.broadcast_to(table[:, k : k + 1], (8, gx)) for k in range(5)]
            to = pl.multiple_of(to_base + g * 8, 8)
            for j in range(nj):
                target[j, pl.ds(to, 8), :] = (
                    w[0] * source[j, pl.ds(at, 8), :]
                    + w[1] * source[j, pl.ds(at + 1, 8), :]
                    + w[2] * source[j, pl.ds(at - 1, 8), :]
                    + w[3] * source[j, pl.ds(at + pitch, 8), :]
                    + w[4] * source[j, pl.ds(at - pitch, 8), :]
                )
            return carry

        lax.fori_loop(0, gx // 8, group, 0, unroll=gx // 8)

    def wrap(source, y):
        base = pl.multiple_of(y * pitch, 8)
        for j in range(nj):
            source[j, pl.ds(base, 8), :] = source[j, pl.ds(base + gx, 8), :]
            source[j, pl.ds(base + 8 + gx, 8), :] = source[j, pl.ds(base + 8, 8), :]

    def loop(low, high, body):
        def step(y, carry):
            body(y)
            return carry

        lax.fori_loop(low, high, step, 0)

    def one_row(y):
        first_row(mid, one, y + 1, y, y * pitch + 8)
        wrap(one, y)

    def two_row(y):
        first_row(one, flat_ref, y + 1, y + 1, y * gx)

    rows(row_from, all_pieces[:urgent], landed)
    corners(col_to, start)
    columns(col_from, landed)
    low, high = min(HALO, ny // 2), max(ny - HALO, ny // 2)
    loop(HALO, HALO + ny, second_rows)
    loop(2, ny, one_row)
    loop(low, high, two_row)
    rows(row_from, all_pieces[urgent:], landed)
    corners(col_from, landed)
    loop(0, HALO, second_rows)
    loop(HALO + ny, 2 * HALO + ny, second_rows)
    loop(0, 2, one_row)
    loop(ny, ny + 2, one_row)
    loop(0, low, two_row)
    loop(high, ny, two_row)

    def pick(k, carry):
        at = obs_ref[jnp.minimum(row_start + k, obs_total - 1)] - row * pts
        at = jnp.clip(at, 0, pts - 1)
        for j in range(nj):
            rows_ref[j, pl.ds(k, 1), :] = flat_ref[j, pl.ds(at, 1), :]
        return carry

    lax.fori_loop(0, rows_ref.shape[1], pick, 0)

    slots = cols_ref.shape[0]
    hots = []
    for j in range(nj):
        lane = lax.broadcasted_iota(jnp.int32, (slots, gx), 1) + j * gx
        hots.append((lane == col_loc[...]).astype(jnp.float32).astype(jnp.bfloat16))
    hot = jnp.concatenate(hots, axis=1)
    dims = (((1,), (1,)), ((), ()))

    def chosen(values):
        high, low = split(jnp.concatenate(values, axis=1))
        return lax.dot_general(
            hot, high, dims, preferred_element_type=jnp.float32
        ) + lax.dot_general(hot, low, dims, preferred_element_type=jnp.float32)

    half = rows_ref.shape[1] // 2
    both = chosen([rows_ref[j] for j in range(nj)])
    for side_of in range(2):
        first = side_of * (half + pts // 2)
        cols_ref[:, first : first + half] = both[:, side_of * half : (side_of + 1) * half]

    def pick_cols(y, carry):
        at = pl.multiple_of(y * gx, gx)
        to = pl.multiple_of(at + jnp.where(2 * y >= ny, 2 * half, half), gx)
        cols_ref[:, pl.ds(to, gx)] = chosen([flat_ref[j, pl.ds(at, gx), :] for j in range(nj)])
        return carry

    lax.fori_loop(0, ny, pick_cols, 0)

    rows(row_to, all_pieces, sent)
    columns(col_to, sent)
    corners(col_to, sent)


def transport(tile, obs_point, winds, max_row, max_col, sizes):
    row_count, col_count, ny, gx, nj = sizes
    pts, edge, pitch = ny * gx, HALO * gx, gx + 16
    grid_y = winds[0].shape[0]
    vmem = pl.BlockSpec(memory_space=pltpu.VMEM)
    return pl.pallas_call(
        functools.partial(transport_kernel, sizes),
        in_specs=[
            pl.BlockSpec(memory_space=pltpu.SMEM),
            pl.BlockSpec(memory_space=pl.ANY),
            vmem,
            vmem,
            vmem,
        ],
        out_specs=[vmem, vmem, vmem],
        out_shape=[
            jax.ShapeDtypeStruct((nj, pts, gx), jnp.float32),
            jax.ShapeDtypeStruct((nj, max_row, gx), jnp.float32),
            jax.ShapeDtypeStruct((max_col, max_row + pts), jnp.float32),
        ],
        scratch_shapes=[
            pltpu.VMEM((pts + 2 * edge, nj, gx), jnp.float32),
            pltpu.VMEM((2 * HALO, pts + 2 * edge, gx), jnp.float32),
            pltpu.VMEM((nj, (ny + 4) * pitch, gx), jnp.float32),
            pltpu.VMEM((nj, (ny + 2) * pitch, gx), jnp.float32),
            pltpu.VMEM(((grid_y + 2) * 8, gx), jnp.float32),
            pltpu.VMEM(((ny + 2) * gx, gx), jnp.float32),
            pltpu.VMEM((5 * (nj + 2), 8, gx), jnp.float32),
            pltpu.VMEM((max_col, gx), jnp.int32),
            pltpu.SemaphoreType.DMA(()),
            pltpu.SemaphoreType.DMA((2, 2, 3)),
            pltpu.SemaphoreType.DMA((2, 2, HALO)),
            pltpu.SemaphoreType.DMA((2, 2, 2, HALO)),
        ],
        compiler_params=pltpu.CompilerParams(
            collective_id=0, has_side_effects=True, vmem_limit_bytes=62 << 20
        ),
    )(obs_point, tile, *winds)


def dot3(left, right):
    l_hi, l_lo = split(left)
    r_hi, r_lo = split(right)
    return (
        jnp.dot(l_hi, r_hi, preferred_element_type=jnp.float32)
        + jnp.dot(l_hi, r_lo, preferred_element_type=jnp.float32)
        + jnp.dot(l_lo, r_hi, preferred_element_type=jnp.float32)
    )


def one_hot(mask):
    return mask.astype(jnp.float32).astype(jnp.bfloat16)


def gather_kernel(
    sizes,
    cols_in,
    rows_in,
    obs_ref,
    var_ref,
    f_ref,
    s_ref,
    peer,
    own,
    up_in,
    down_in,
    up_out,
    down_out,
    parts,
    pairs,
    power,
    inverse,
    wide,
    peer_sem,
    rows_sem,
    up_sem,
    down_sem,
    pair_sem,
    twin_sem,
    half_sem,
):
    row_count, col_count, ny, gx, nj = sizes
    row, col = lax.axis_index("row"), lax.axis_index("col")
    pts = ny * gx
    place, core = col // 2, lax.rem(col, 2)
    places = col_count // 2
    twin = col + 1 - 2 * core
    chunks, total = own.shape[0], 2 * own.shape[1]
    ahead = chunks - pts // gx
    width = chunks // 2 * gx
    below, above = place > 0, place < places - 1

    barrier = pltpu.get_barrier_semaphore()
    waits = row_count + below.astype(jnp.int32) + above.astype(jnp.int32)

    def greet(target):
        pl.semaphore_signal(barrier, inc=1, device_id=target, device_id_type=MESH)

    greet((row, twin))
    for hop in range(1, row_count):
        greet((lax.rem(row + hop, row_count), col))
    pl.when(below)(lambda: greet((row, col - 2)))
    pl.when(above)(lambda: greet((row, col + 2)))
    pl.semaphore_wait(barrier, waits)

    def remote(src, dst, sems, index, target):
        return pltpu.make_async_remote_copy(
            src_ref=src,
            dst_ref=dst,
            send_sem=sems.at[(0, *index)],
            recv_sem=sems.at[(1, *index)],
            device_id=target,
            device_id_type=MESH,
        )

    other = pl.multiple_of((1 - core) * width, gx)
    swap = remote(cols_in.at[:, pl.ds(other, width)], peer, peer_sem, (), (row, twin))
    swap.start()

    def rows_copy(hop):
        return remote(
            rows_in, parts.at[row], rows_sem, (hop - 1,), (lax.rem(row + hop, row_count), col)
        )

    def rows_landed(hop):
        source = lax.rem(row + row_count - hop, row_count)
        return remote(rows_in, parts.at[source], rows_sem, (hop - 1,), (source, col))

    for hop in range(1, row_count):
        rows_copy(hop).start()
    parts[row] = rows_in[...]

    points = obs_ref[...]
    ids = lax.broadcasted_iota(jnp.int32, (1, total), 1).astype(jnp.float32)

    def before(limit):
        return jnp.sum((points < limit).astype(jnp.float32), axis=1, keepdims=True)

    def within(block):
        size = nj * gx
        here = (points >= block * size) & (points < (block + 1) * size)
        return jnp.where(here, ids - before(block * size), -1.0)

    slot_across = ids
    max_row = rows_in.shape[1]
    for r in range(1, row_count):
        fewer = before(r * pts) - before((r - 1) * pts)
        slot_across = slot_across + jnp.where(points >= r * pts, max_row - fewer, 0.0)
    stack = jnp.concatenate(
        [within(col), within(twin), slot_across, jnp.zeros((gx - 3, total), jnp.float32)], axis=0
    ).T
    slot_down = stack[:, 2:3]
    lanes = lax.broadcasted_iota(jnp.int32, (total, cols_in.shape[0]), 1).astype(jnp.float32)
    mine_hot = one_hot(lanes == stack[:, 0:1])
    peer_hot = one_hot(lanes == stack[:, 1:2])
    first = pl.multiple_of(core * width, gx)
    swap.wait_recv()

    def placed(hot, value):
        high, low = split(value)
        return jnp.dot(hot, high, preferred_element_type=jnp.float32) + jnp.dot(
            hot, low, preferred_element_type=jnp.float32
        )

    for piece in range(chunks // 2):
        at = pl.multiple_of(first + piece * gx, gx)
        value = placed(mine_hot, cols_in[:, pl.ds(at, gx)]) + placed(
            peer_hot, peer[:, piece * gx : (piece + 1) * gx]
        )
        own[2 * piece] = value[: total // 2]
        own[2 * piece + 1] = value[total // 2 :]

    @pl.when(jnp.logical_not(below))
    def _():
        up_in[...] = jnp.zeros_like(up_in)

    @pl.when(jnp.logical_not(above))
    def _():
        down_in[...] = jnp.zeros_like(down_in)

    def up_copy(chunk):
        return remote(up_out.at[chunk], up_in.at[chunk], up_sem, (chunk,), (row, col + 2))

    def down_copy(chunk):
        return remote(down_out.at[chunk], down_in.at[chunk], down_sem, (chunk,), (row, col - 2))

    def pair_copy(index, hop):
        return remote(
            pairs.at[row, core, index],
            pairs.at[row, core, index],
            pair_sem,
            (index, hop - 1),
            (lax.rem(row + hop, row_count), col),
        )

    def pair_landed(index, hop):
        source = lax.rem(row + row_count - hop, row_count)
        ref = pairs.at[source, core, index]
        return remote(ref, ref, pair_sem, (index, hop - 1), (source, col))

    def twin_copy(index, hop):
        source = lax.rem(row + row_count - hop, row_count)
        ref = pairs.at[source, core, index]
        return remote(ref, ref, twin_sem, (index, hop), (row, twin))

    def twin_landed(index, hop):
        source = lax.rem(row + row_count - hop, row_count)
        ref = pairs.at[source, 1 - core, index]
        return remote(ref, ref, twin_sem, (index, hop), (row, twin))

    def half_copy(chunk):
        ref = f_ref.at[core * (chunks - ahead) + chunk]
        return remote(ref, ref, half_sem, (chunk,), (row, twin))

    def half_landed(chunk):
        ref = f_ref.at[(1 - core) * (chunks - ahead) + chunk]
        return remote(ref, ref, half_sem, (chunk,), (row, twin))

    def up_stage(chunk):
        @pl.when(below)
        def _():
            up_copy(chunk).wait_recv()

        @pl.when(above)
        def _():
            up_out[chunk] = up_in[chunk] + own[chunk]
            up_copy(chunk).start()

    def down_stage(chunk):
        @pl.when(above)
        def _():
            down_copy(chunk).wait_recv()

        @pl.when(below)
        def _():
            down_out[chunk] = down_in[chunk] + own[chunk]
            down_copy(chunk).start()

    def finish(chunk):
        value = up_in[chunk] + own[chunk] + down_in[chunk]

        @pl.when(chunk < ahead)
        def _():
            pairs[row, core, chunk] = value
            for hop in range(1, row_count):
                pair_copy(chunk, hop).start()
            twin_copy(chunk, 0).start()

        @pl.when(chunk >= ahead)
        def _():
            f_ref[core * (chunks - ahead) + chunk - ahead] = value
            half_copy(chunk - ahead).start()

    def relay():
        for index in range(ahead):
            for hop in range(1, row_count):
                pair_landed(index, hop).wait_recv()
                twin_copy(index, hop).start()

    half = ahead // 2 * gx
    slots = row_count * 2 * half

    def twins():
        for index in range(ahead):
            for hop in range(row_count):
                twin_landed(index, hop).wait_recv()

    def gathered():
        innovation = None
        for r in range(row_count):
            values = [
                jnp.concatenate([pairs[r, q, 2 * k], pairs[r, q, 2 * k + 1]], axis=0)
                for q in range(2)
                for k in range(ahead // 2)
            ]
            high, low = split(jnp.concatenate(values, axis=1))
            at = lax.broadcasted_iota(jnp.int32, (2 * half, total), 0) + r * 2 * half
            hot = one_hot(at.astype(jnp.float32) == slot_across)
            term = jnp.dot(high, hot, preferred_element_type=jnp.float32) + jnp.dot(
                low, hot, preferred_element_type=jnp.float32
            )
            innovation = term if innovation is None else innovation + term
        diagonal = lax.broadcasted_iota(jnp.int32, (total, total), 0) == lax.broadcasted_iota(
            jnp.int32, (total, total), 1
        )
        eye = diagonal.astype(jnp.float32)
        innovation = innovation + jnp.where(diagonal, var_ref[...], 0.0)
        power[...] = eye - innovation / newton_scale
        inverse[...] = (eye + power[...]) / newton_scale

    def square():
        power[...] = dot3(power[...], power[...])

    def sweep():
        inverse[...] = inverse[...] + dot3(inverse[...], power[...])

    def widen():
        at = lax.broadcasted_iota(jnp.int32, (total, slots), 1).astype(jnp.float32)
        wide[...] = placed_right(inverse[...], one_hot(at == slot_down))

    work = [relay, twins, gathered] + [square, sweep] * (NS_ITERS - 1) + [widen]

    from_below, from_above = LAG * place, LAG * (places - 1 - place)
    for tick in range(chunks + LAG * (places - 1)):
        for stage, lag in (
            (up_stage, from_below),
            (down_stage, from_above),
            (finish, jnp.maximum(from_below, from_above)),
        ):
            chunk = tick - lag

            @pl.when((chunk >= 0) & (chunk < chunks))
            def _(stage=stage, chunk=chunk):
                stage(chunk)

        if tick >= FIRST_WORK and work:
            work.pop(0)()
    for task in work:
        task()
    for hop in range(1, row_count):
        rows_landed(hop).wait_recv()
    step = min(2, nj)
    for j in range(0, nj, step):
        right = jnp.concatenate(
            [parts[:, j + k].reshape(slots, gx) for k in range(step)], axis=1
        )
        value = dot3(wide[...], right)
        for k in range(step):
            s_ref[j + k] = value[:, k * gx : (k + 1) * gx]

    for chunk in range(chunks - ahead):
        half_landed(chunk).wait_recv()
        half_copy(chunk).wait_send()
    swap.wait_send()
    for hop in range(1, row_count):
        rows_copy(hop).wait_send()
    for index in range(ahead):
        for hop in range(1, row_count):
            pair_copy(index, hop).wait_send()
        for hop in range(row_count):
            twin_copy(index, hop).wait_send()
    for chunk in range(chunks):
        pl.when(above)(lambda: up_copy(chunk).wait_send())
        pl.when(below)(lambda: down_copy(chunk).wait_send())


def placed_right(value, hot):
    high, low = split(value)
    return jnp.dot(high, hot, preferred_element_type=jnp.float32) + jnp.dot(
        low, hot, preferred_element_type=jnp.float32
    )


def gather(cols_part, rows_part, obs_point, var, sizes):
    row_count, col_count, ny, gx, nj = sizes
    pts, total = ny * gx, var.shape[0]
    max_col, max_row = cols_part.shape[0], rows_part.shape[1]
    ahead = max_row // gx
    chunks = ahead + pts // gx
    vmem = pl.BlockSpec(memory_space=pltpu.VMEM)
    dma = pltpu.SemaphoreType.DMA
    f32 = jnp.float32
    return pl.pallas_call(
        functools.partial(gather_kernel, sizes),
        in_specs=[vmem] * 4,
        out_specs=[vmem, vmem],
        out_shape=[
            jax.ShapeDtypeStruct((2 * pts // gx, total // 2, gx), f32),
            jax.ShapeDtypeStruct((nj, total, gx), f32),
        ],
        scratch_shapes=[
            pltpu.VMEM((max_col, chunks // 2 * gx), f32),
            pltpu.VMEM((chunks, total // 2, gx), f32),
            pltpu.VMEM((chunks, total // 2, gx), f32),
            pltpu.VMEM((chunks, total // 2, gx), f32),
            pltpu.VMEM((chunks, total // 2, gx), f32),
            pltpu.VMEM((chunks, total // 2, gx), f32),
            pltpu.VMEM((row_count, nj, max_row, gx), f32),
            pltpu.VMEM((row_count, 2, ahead, total // 2, gx), f32),
            pltpu.VMEM((total, total), f32),
            pltpu.VMEM((total, total), f32),
            pltpu.VMEM((total, row_count * max_row), f32),
            dma((2,)),
            dma((2, row_count - 1)),
            dma((2, chunks)),
            dma((2, chunks)),
            dma((2, ahead, row_count - 1)),
            dma((2, ahead, row_count)),
            dma((2, chunks - ahead)),
        ],
        compiler_params=pltpu.CompilerParams(
            collective_id=1, has_side_effects=True, vmem_limit_bytes=60 << 20
        ),
    )(cols_part, rows_part, obs_point[None, :], var[None, :])


def update_kernel(nj, gx, rows, flat_ref, left_ref, right_ref, out_ref):
    left = jnp.concatenate([left_ref[k].T for k in range(left_ref.shape[0])], axis=0)
    l_hi, l_lo = split(left)
    wide = min(2, nj)
    for j in range(0, nj, wide):
        r_hi, r_lo = split(
            jnp.concatenate([right_ref[j + k] for k in range(wide)], axis=1)
        )
        total = (
            jnp.dot(l_hi, r_hi, preferred_element_type=jnp.float32)
            + jnp.dot(l_hi, r_lo, preferred_element_type=jnp.float32)
            + jnp.dot(l_lo, r_hi, preferred_element_type=jnp.float32)
        )
        for k in range(wide):
            out_ref[:, j + k, :] = flat_ref[j + k] - total[:, k * gx : (k + 1) * gx]


def update(flat, left, right, rows):
    nj, pts, gx = flat.shape
    depth = left.shape[1]
    return pl.pallas_call(
        functools.partial(update_kernel, nj, gx, rows),
        grid=(pts // rows,),
        in_specs=[
            pl.BlockSpec((nj, rows, gx), lambda i: (0, i, 0)),
            pl.BlockSpec((rows // gx, depth, gx), lambda i: (i, 0, 0)),
            pl.BlockSpec((nj, depth, gx), lambda i: (0, 0, 0)),
        ],
        out_specs=pl.BlockSpec((rows, nj, gx), lambda i: (i, 0, 0)),
        out_shape=jax.ShapeDtypeStruct((pts, nj, gx), jnp.float32),
        compiler_params=pltpu.CompilerParams(vmem_limit_bytes=48 << 20),
    )(flat, left, right)


def on_device(covariance, wind_x, wind_y, diffusivity, obs_point, obs_var):
    ny, gx, nj, _ = covariance.shape
    row_count, col_count = lax.axis_size("row"), lax.axis_size("col")
    rows_dev = ny * gx
    sizes = (row_count, col_count, ny, gx, nj)
    obs_total = obs_point.shape[0]
    tile = covariance.reshape(rows_dev, nj, gx)

    max_row = max(2 * gx, 2 * obs_total // row_count)
    max_col = max(gx, 2 * obs_total // col_count)
    winds = (wind_x, wind_y, diffusivity)
    flat, rows_part, cols_part = transport(tile, obs_point, winds, max_row, max_col, sizes)
    columns, scaled = gather(cols_part, rows_part, obs_point, obs_var, sizes)
    columns = columns.reshape(rows_dev // gx, obs_total, gx)
    analysis = update(flat, columns, scaled, min(256, rows_dev))
    return analysis.reshape(ny, gx, nj, gx)


def solution(mesh):
    in_specs = (P("row", None, "col", None), P(), P(), P(), P(), P())
    out_specs = P("row", None, "col", None)
    return jax.shard_map(
        on_device, mesh=mesh, in_specs=in_specs, out_specs=out_specs, check_vma=False
    )
```
